32 devices in a mesh: groups: 2 (over x), patch: 16 (over z, y, core).
Axes of the slice: x: 2, y: 2, z: 4, core: 2. Of those that a mesh axis runs over, the one named last changes fastest.
Arguments:
- template: float32 [64, 32768], P(None, ('groups', 'patch')), parts along dimension 1, may hold values from -6 to 6
- science: float32 [512, 4, 128], P(('groups', 'patch')), parts along dimension 0, may hold values from -6 to 6
- dest: int32 [512, 1], P(('groups', 'patch')), parts along dimension 0, may hold values from 0 to 15; in each aligned block of 16 rows (0 to 15, 16 to 31, ...) at most 2 rows name the same one
- row_offset: int32 [512], P(('groups', 'patch')), parts along dimension 0, may hold values from 0 to 60
- col_block: int32 [512], P(('groups', 'patch')), parts along dimension 0, may hold values from 0 to 7
- basis_rows: float32 [27, 21], replicated, may hold values from -1.25 to 1.25
- basis_cols: float32 [27, 21], replicated, may hold values from -1.25 to 1.25
- stamp_rows: int32 [32, 24], P('groups'), parts along dimension 0, may hold values from 0 to 63
- stamp_cols: int32 [32, 24], P('groups'), parts along dimension 0, may hold values from 0 to 1023
Outputs:
- difference: float32 [512, 4, 128], P(('groups', 'patch')), parts along dimension 0
The draws below stay inside these ranges and needn't reach their ends.
There are 2 independent parts, one for each index of `groups`. The reference program is written for one: setup_inputs(seed, part) draws one part's arguments, and reference() takes and returns one part's arrays. A program takes and returns all parts, laid end to end along the dimension named above; an argument that names none is the same for every part. Nothing has to cross between parts.
Inputs may be any that keep to these rules, and one draw needn't show every extreme that they name: `dest`: each visit sends at most 2 strips to one sub-patch, and in every draw some visit sends exactly 2 to one.
All inputs are finite; a program needn't handle non-finite values.
Results may differ from the reference program's by a relative error of at most 0.0003.
Values sent between devices are 32-bit elements; how exact they have to be, the bound alone decides.
No kernel may reach another device: no remote copies, remote signals or barrier semaphores. Data moves between devices by JAX's collectives and lax.ppermute only.
A program may use at most 64 MiB of HBM per device.

```python
import math
import jax
import jax.numpy as jnp
import numpy as np
from jax import lax

BASES = 27
TAPS = 21
BLOCK = 128
CAP = 2
STAMPS = 24
STAMP_HALF = 10
STRIP_ROWS = 4
SUB_ROWS = 64
SUB_COLS = 1024
STRIPS = 16
TOTAL_STRIPS = 256
N_PATCH = 16


def plant(values, stream_key, least, high):
    shape = values.shape
    spot = [jax.random.randint(jax.random.fold_in(stream_key, axis), (), 0, shape[axis]) for axis in range(len(shape))]
    values = values.at[tuple(spot)].set(least)
    longest = shape.index(max(shape))
    spot[longest] = (spot[longest] + 1) % shape[longest]
    return values.at[tuple(spot)].set(high)


def block_levels(rng, extent, shards, least, high):
    factor_of, own = 1.0, jax.random.fold_in(rng, 6)
    for axis_at, shards_of in shards:
        heights = jnp.exp(jax.random.uniform(jax.random.fold_in(own, axis_at), (shards_of,), jnp.float32, least / len(shards), high / len(shards)))
        factor_of = factor_of * jnp.repeat(heights, extent[axis_at] // shards_of).reshape([-1 if axis == axis_at else 1 for axis in range(len(extent))])
    return factor_of


def shared_out(stream_key, own, number, rows, amount, top, limit, slope):
    sequence = jax.random.permutation(stream_key, amount)
    packed, common = portions_of(amount, rows * top, limit, slope, True), portions_of(amount, rows * top, limit, slope, False)
    places = jnp.arange(amount)

    def named(lengths, rotation):
        used = int((lengths > 0).sum())
        fixed = max(1, used // 4)
        passed = fixed + (places - fixed + rotation * (used - fixed)) % max(1, amount - fixed)
        return jnp.zeros((amount,), jnp.int32).at[sequence[jnp.where(places < fixed, places, passed)]].set(jnp.asarray(lengths, jnp.int32))

    lengths = jnp.where(number % 4 == 0, named(packed, number // 4), named(common, number - number // 4 - 1))
    mixed = jax.random.permutation(jax.random.fold_in(own, 3), amount)
    donor, sink = mixed[0:amount // 2 * 2:2], mixed[1:amount // 2 * 2:2]
    slack = jnp.minimum(lengths[donor] - 1, limit - lengths[sink]) // 2
    slack = jnp.where((donor == sequence[0]) | (sink == sequence[0]) | (lengths[sink] == 0), 0, jnp.maximum(slack, 0))
    passed = jax.random.randint(jax.random.fold_in(own, 4), (amount // 2,), 0, 1 << 20) % (slack + 1)
    lengths = lengths.at[donor].add(-passed).at[sink].add(passed)
    items = jnp.searchsorted(jnp.cumsum(lengths), jnp.arange(rows * top), side="right").astype(jnp.int32)
    listing = items.reshape(top, rows).T
    listing = listing[jax.random.permutation(jax.random.fold_in(own, 1), rows)]
    rotation = jax.random.randint(jax.random.fold_in(own, 2), (rows, 1), 0, top)
    return jnp.take_along_axis(listing, (jnp.arange(top)[None, :] + rotation) % top, axis=1)


def portions_of(count, total, limit, skew, full):
    weights = [(1 << 20) // math.isqrt(grade ** skew) + 1 for grade in range(1, count + 1)]
    largest = limit if full else min(limit, max(-(-total // count), total * weights[0] // sum(weights)))
    least = 1 if total - largest >= count - 1 else 0
    holding, spare = [largest] + [least] * (count - 1), total - largest - least * (count - 1)
    while spare > 0:
        movable = [i for i in range(1, count) if holding[i] < largest] or [i for i in range(1, count) if holding[i] < limit]
        pool, remaining = sum([weights[i] for i in movable]), spare
        for i in movable:
            extra = min(limit - holding[i], max(1, remaining * weights[i] // pool), spare)
            holding[i] = holding[i] + extra
            spare = spare - extra
    return np.array(holding)


def normal_values(own_key, shape, scale, bound, split=(), kind=jnp.bfloat16):
    array = scale * jax.random.normal(own_key, shape, jnp.float32)
    if split:
        array = array * block_levels(own_key, shape, split, -0.22, 0.18)
    return jnp.clip(array, -bound, bound).astype(kind)


def setup_inputs(seed: int = 0, part: int = 0) -> dict:
    key_of = jax.random.split(jax.random.key(seed), 10)
    own_keys = jax.random.split(jax.random.fold_in(key_of[9], part), 10)
    template = normal_values(own_keys[0], (SUB_ROWS, N_PATCH * SUB_COLS), 1.0, 6.0, ((1, 16),), jnp.float32)
    science = normal_values(own_keys[1], (TOTAL_STRIPS, STRIP_ROWS, BLOCK), 1.0, 6.0, ((0, 16),), jnp.float32)
    dest_keys = jax.random.split(jax.random.fold_in(own_keys[2], 1), TOTAL_STRIPS // STRIPS)
    dest_turns = jax.random.permutation(jax.random.fold_in(own_keys[2], 3), TOTAL_STRIPS // STRIPS)
    dest = jax.vmap(lambda own, number: shared_out(jax.random.fold_in(own_keys[2], 2), own, number, STRIPS, N_PATCH, 1, CAP, 2))(dest_keys, dest_turns).reshape((TOTAL_STRIPS, 1))
    row_offset = plant(jax.random.randint(own_keys[3], (TOTAL_STRIPS,), 0, SUB_ROWS - STRIP_ROWS + 1), jax.random.fold_in(own_keys[3], 1), 0, SUB_ROWS - STRIP_ROWS).astype(jnp.int32)
    col_block = plant(jax.random.randint(own_keys[4], (TOTAL_STRIPS,), 0, SUB_COLS // BLOCK), jax.random.fold_in(own_keys[4], 1), 0, (SUB_COLS // BLOCK) - 1).astype(jnp.int32)
    basis_rows = normal_values(key_of[5], (BASES, TAPS), TAPS ** -0.5, 1.25, (), jnp.float32)
    basis_cols = normal_values(key_of[6], (BASES, TAPS), TAPS ** -0.5, 1.25, (), jnp.float32)
    stamp_rows = plant(jax.random.randint(own_keys[7], (N_PATCH, STAMPS), 0, SUB_ROWS), jax.random.fold_in(own_keys[7], 1), 0, SUB_ROWS - 1).astype(jnp.int32)
    stamp_cols = plant(jax.random.randint(own_keys[8], (N_PATCH, STAMPS), 0, SUB_COLS), jax.random.fold_in(own_keys[8], 1), 0, SUB_COLS - 1).astype(jnp.int32)
    return dict(template=template, science=science, dest=dest, row_offset=row_offset, col_block=col_block, basis_rows=basis_rows, basis_cols=basis_cols, stamp_rows=stamp_rows, stamp_cols=stamp_cols)


HIGH = lax.Precision.HIGHEST
RIDGE = 1.0

def filter_field(padded, row_taps, col_taps):
    taps = row_taps.shape[0]
    out_rows = padded.shape[0] - taps + 1
    out_cols = padded.shape[1] - taps + 1
    across = jnp.zeros((padded.shape[0], out_cols), jnp.float32)
    for shift_tap in range(taps):
        across = across + col_taps[shift_tap] * padded[:, shift_tap:shift_tap + out_cols]
    result = jnp.zeros((out_rows, out_cols), jnp.float32)
    for shift_tap in range(taps):
        result = result + row_taps[shift_tap] * across[shift_tap:shift_tap + out_rows, :]
    return result

def stamp_mask(row_start, blocks, stamp_r, stamp_c):
    rows_here = row_start[:, None] + jnp.arange(STRIP_ROWS, dtype=jnp.int32)[None, :]
    cols_here = blocks[:, None] * BLOCK + jnp.arange(BLOCK, dtype=jnp.int32)[None, :]
    row_hit = (jnp.abs(rows_here[:, :, None] - stamp_r[:, None, :]) <= STAMP_HALF).astype(jnp.float32)
    col_hit = (jnp.abs(stamp_c[:, :, None] - cols_here[:, None, :]) <= STAMP_HALF).astype(jnp.float32)
    counts = jnp.einsum('nis,nsj->nij', row_hit, col_hit, precision=HIGH)
    return jnp.minimum(counts, 1.0)

def cholesky_solve(matrix, rhs):
    factor = jnp.linalg.cholesky(matrix)
    inner = lax.linalg.triangular_solve(factor, rhs[..., None], left_side=True, lower=True)
    return lax.linalg.triangular_solve(factor, inner, left_side=True, lower=True, transpose_a=True)[..., 0]

def reference(template, science, dest, row_offset, col_block, basis_rows, basis_cols, stamp_rows, stamp_cols):
    half_taps = (TAPS - 1) // 2
    padded = jnp.pad(template, ((half_taps, half_taps), (half_taps, half_taps)))

    def one_basis(filters):
        return filter_field(padded, filters[0], filters[1])
    conv = lax.map(one_basis, (basis_rows, basis_cols))
    targets_all = dest[:, 0].astype(jnp.int32)

    def one_visit(visit):
        start = (visit * STRIPS).astype(jnp.int32)
        targets = lax.dynamic_slice_in_dim(targets_all, start, STRIPS)
        row_start = lax.dynamic_slice_in_dim(row_offset, start, STRIPS).astype(jnp.int32)
        blocks = lax.dynamic_slice_in_dim(col_block, start, STRIPS).astype(jnp.int32)
        pixels = lax.dynamic_slice_in_dim(science, start, STRIPS).reshape(STRIPS, -1)

        def window_of(target, first_row, block):
            return lax.dynamic_slice(conv, (jnp.int32(0), first_row, target * SUB_COLS + block * BLOCK), (BASES, STRIP_ROWS, BLOCK))
        windows = jax.vmap(window_of)(targets, row_start, blocks).reshape(STRIPS, BASES, -1)
        design = jnp.concatenate([windows, jnp.ones((STRIPS, 1, windows.shape[2]), jnp.float32)], axis=1)
        weight = stamp_mask(row_start, blocks, stamp_rows[targets], stamp_cols[targets]).reshape(STRIPS, 1, -1)
        weighted = design * weight
        normal = jnp.einsum('skp,slp->skl', weighted, design, precision=HIGH)
        moment = jnp.einsum('skp,sp->sk', weighted, pixels, precision=HIGH)
        owner_hot = (targets[:, None] == jnp.arange(N_PATCH, dtype=jnp.int32)[None, :]).astype(jnp.float32)
        columns = BASES + 1
        group_normal = jnp.einsum('sp,skl->pkl', owner_hot, normal, precision=HIGH) + RIDGE * jnp.eye(columns, dtype=jnp.float32)
        group_moment = jnp.einsum('sp,sk->pk', owner_hot, moment, precision=HIGH)
        coefficients = cholesky_solve(group_normal, group_moment)
        strip_coeff = jnp.einsum('sp,pk->sk', owner_hot, coefficients, precision=HIGH)
        model_image = jnp.einsum('skp,sk->sp', design, strip_coeff, precision=HIGH)
        return (pixels - model_image).reshape(STRIPS, STRIP_ROWS, BLOCK)
    result = lax.map(one_visit, jnp.arange(N_PATCH, dtype=jnp.int32))
    return result.reshape(N_PATCH * STRIPS, STRIP_ROWS, BLOCK)
```

```python
import jax
import jax.numpy as jnp
from jax import lax
from jax.experimental import pallas as pl
from jax.experimental.pallas import tpu as pltpu
from jax.sharding import PartitionSpec as P

CAP = 2
STAMP_HALF = 10
RIDGE = 1.0
LANES = 128
SUBS = 8
VISITS = 16

F32 = jnp.float32
BF16 = jnp.bfloat16
NT = (((1,), (1,)), ((), ()))


def iota(shape, dim):
    return lax.broadcasted_iota(jnp.int32, shape, dim)


def split(x):
    high = x.astype(BF16)
    return high, (x - high.astype(F32)).astype(BF16)


INFO_ROW = 2


def pack_kernel(own_ref, dest_ref, row_ref, col_ref, first_ref, last_ref, science_ref, out_ref, count, source):
    peers = out_ref.shape[0]
    strips = science_ref.shape[0]
    own = own_ref[0]

    def clear(d, _):
        count[d] = 0
        for r in range(CAP):
            source[CAP * d + r] = -1
        return 0

    lax.fori_loop(0, peers, clear, 0, unroll=min(peers, 16))

    def place(s, _):
        d = dest_ref[s, 0]
        rank = count[d]
        source[CAP * d + rank] = s
        count[d] = rank + 1
        return 0

    lax.fori_loop(0, strips, place, 0, unroll=min(strips, 16))

    edges = jnp.concatenate([first_ref[...], last_ref[...]], axis=0).T
    lane = iota((SUBS, LANES), 1)
    sub = iota((SUBS, LANES), 0)
    rows = LANES // 2
    low = lane < rows
    head = jnp.where(low, edges[0:8], pltpu.roll(edges[8:16], rows, 1))
    tail = jnp.where(low, pltpu.roll(edges[120:128], rows, 1), edges[112:120])
    info_here = (~low) & (sub == INFO_ROW)

    def fill(d, _):
        halo = jnp.where(d == own + 1, tail, head)
        info = jnp.zeros((SUBS, LANES), F32)
        parts = []
        for r in range(CAP):
            s = source[CAP * d + r]
            live = s >= 0
            at = jnp.maximum(s, 0)
            strip = science_ref[at]
            parts.append(jnp.where(live, strip, 0.0))
            values = (row_ref[at], col_ref[at], jnp.int32(1))
            for j, value in enumerate(values):
                value = jnp.where(live, value, 0).astype(F32)
                info = jnp.where(lane == rows + 3 * r + j, value, info)
        out_ref[d, 0:SUBS, :] = jnp.concatenate(parts, axis=0)
        out_ref[d, SUBS : 2 * SUBS, :] = jnp.where(info_here, info, halo)
        return 0

    lax.fori_loop(0, peers, fill, 0, unroll=min(peers, 16))


def prep_kernel(own_ref, rows_ref, cols_ref, stamp_r_ref, stamp_c_ref, col_taps_ref, row_taps_ref, mask_ref, pad_c, pad_r):
    bases, taps = rows_ref.shape
    own = own_ref[0]
    blocks, sub_rows, _ = mask_ref.shape
    sub_rows = sub_rows - SUBS
    sub_cols = blocks * LANES
    centre_r = stamp_r_ref[pl.ds(own, 1), :]
    centre_c = stamp_c_ref[pl.ds(own, 1), :]
    stamps = centre_r.shape[1]
    row_hit = (jnp.abs(iota((sub_rows, stamps), 0) - centre_r) <= STAMP_HALF).astype(F32).astype(BF16)
    col_hit = (jnp.abs(iota((sub_cols, stamps), 0) - centre_c) <= STAMP_HALF).astype(F32).astype(BF16)
    counts = lax.dot_general(row_hit, col_hit, NT, preferred_element_type=F32)
    for c in range(blocks):
        mask_ref[c, 0:sub_rows, :] = jnp.minimum(counts[:, LANES * c : LANES * (c + 1)], 1.0)
        mask_ref[c, sub_rows:, :] = jnp.zeros((SUBS, LANES), F32)
    pad_c[...] = jnp.zeros_like(pad_c)
    pad_r[...] = jnp.zeros_like(pad_r)
    pad_c[0:bases, 0:taps] = cols_ref[...]
    pad_r[0:bases, 0:taps] = rows_ref[...]
    full = pad_r[...]
    high = full.astype(BF16).astype(F32)
    base = high + pltpu.roll(high, 32, 1) + pltpu.roll(full - high, 64, 1)
    wide = jnp.concatenate([base, jnp.zeros_like(base)], axis=1)
    lower = iota((SUBS, 2 * LANES), 0) < SUBS // CAP
    for k in range(bases):
        row = jnp.broadcast_to(wide[k : k + 1, :], (SUBS, 2 * LANES))
        row = pltpu.roll(row, 0, 1, stride=1, stride_axis=0)
        row = jnp.where(lower, row, pltpu.roll(row, 96 - SUBS // CAP, 1))
        row_taps_ref[SUBS * k : SUBS * (k + 1), :] = row
    row_at = iota((LANES, LANES), 0)
    lane_at = iota((LANES, LANES), 1)
    inside = lane_at >= row_at

    def column(k, _):
        ring = jnp.broadcast_to(pad_c[pl.ds(k, 1), :], (LANES, LANES))
        ring = pltpu.roll(ring, 0, 1, stride=1, stride_axis=0)
        for half, kept in ((0, inside), (1, ~inside)):
            piece_h, piece_l = split(jnp.where(kept, ring, 0.0))
            col_taps_ref[k, 0:LANES, LANES * half : LANES * (half + 1)] = piece_h
            col_taps_ref[k, LANES : 2 * LANES, LANES * half : LANES * (half + 1)] = piece_l
        return 0

    lax.fori_loop(0, bases, column, 0, unroll=3)


def main_kernel(
    own_ref, arrived_ref, left_ref, right_ref, template_ref, col_taps_hbm, row_taps_ref, mask_ref, out_ref,
    frame, info_v, info_s, taps_v, weight, field, design, weighted, gram, copy_sem, taps_sem,
):
    step = pl.program_id(0)
    own = own_ref[0]
    peers = own_ref[1]
    bases = col_taps_hbm.shape[0]
    columns = bases + 1
    rows = template_ref.shape[0]
    blocks = template_ref.shape[1] // LANES
    per = VISITS * SUBS

    info_v[...] = arrived_ref[:, SUBS + INFO_ROW, :]
    info_copy = pltpu.make_async_copy(info_v, info_s, copy_sem)
    info_copy.start()

    @pl.when(step == 0)
    def _():
        taps_copy = pltpu.make_async_copy(col_taps_hbm, taps_v, taps_sem)
        taps_copy.start()
        lane = iota((SUBS, LANES), 1)
        left = jnp.where(own > 0, left_ref[0], 0.0)
        right = jnp.where(own < peers - 1, right_ref[0], 0.0)
        gap = jnp.zeros((LANES - 4 * SUBS, LANES), F32)
        halo = jnp.concatenate([pltpu.roll(right, 64, 1), right, gap, pltpu.roll(left, 64, 1), left], axis=0).T
        frame[:, 0:16, :] = jnp.zeros((blocks + 1, 16, LANES), F32)
        frame[:, 16 + rows :, :] = jnp.zeros((blocks + 1, frame.shape[1] - 16 - rows, LANES), F32)
        shift = 10
        for t in range(rows // SUBS):
            at = slice(SUBS * t, SUBS * (t + 1))
            before = pltpu.roll(halo[at], shift, 1)
            for c in range(blocks + 1):
                if c < blocks:
                    here = template_ref[at, LANES * c : LANES * (c + 1)]
                else:
                    here = halo[rows + SUBS * t : rows + SUBS * (t + 1)]
                here = pltpu.roll(here, shift, 1)
                frame[c, 16 + SUBS * t : 16 + SUBS * (t + 1), :] = jnp.where(lane < shift, before, here)
                before = here
        design[bases, :, :] = jnp.ones((per, LANES), F32)
        weighted[columns + 1 :, :, :] = jnp.zeros((32 - columns - 1, per, LANES), F32)
        taps_copy.wait()

    info_copy.wait()
    row_taps = row_taps_ref[...].astype(BF16)[:, 0:192]

    def convolve_rows(pair, _):
        outs = []
        for half in range(2):
            b = 2 * pair + half
            terms = []
            masks = []
            for r in range(CAP):
                first = info_s[b, 64 + 3 * r].astype(jnp.int32)
                block = info_s[b, 65 + 3 * r].astype(jnp.int32)
                live = info_s[b, 66 + 3 * r]
                sides = [frame[block + side, pl.ds(first + 6, 32), :] for side in range(2)]
                window = jnp.concatenate(sides, axis=1)
                high, low = split(window)
                terms += [high, low, high]
                masks.append(mask_ref[block, pl.ds(first, SUBS), :][0 : SUBS // CAP] * live)
            weight[pl.ds(pl.multiple_of(SUBS * b, SUBS), SUBS), :] = jnp.concatenate(masks, axis=0)
            tall = jnp.concatenate(terms, axis=0)
            across = lax.dot_general(row_taps, tall, (((1,), (0,)), ((), ())), preferred_element_type=F32)
            outs.append(across.reshape(bases, SUBS, 2 * LANES))
        both = jnp.concatenate(outs, axis=1)
        high, low = split(both)
        at = pl.multiple_of(2 * SUBS * pair, 2 * SUBS)
        field[:, pl.ds(at, 2 * SUBS), :] = high
        field[:, pl.ds(per + at, 2 * SUBS), :] = low
        return 0

    lax.fori_loop(0, VISITS // 2, convolve_rows, 0)

    hits = weight[...]

    def convolve_cols(k, _):
        out = lax.dot_general(field[k], taps_v[k], NT, preferred_element_type=F32)
        conv = (out[0:per, LANES:] + out[per:, 0:LANES]) + out[0:per, 0:LANES]
        design[k] = conv
        weighted[k] = conv * hits
        return 0

    lax.fori_loop(0, bases, convolve_cols, 0, unroll=3)
    science = arrived_ref[:, 0:SUBS, :].reshape(per, LANES)
    weighted[bases] = hits
    weighted[columns] = science * hits

    def gram_of(b, _):
        rows_of = []
        for q in range(SUBS):
            rows_of.append(weighted[:, SUBS * b + q, :])
        flat = jnp.concatenate(rows_of, axis=1)
        high, low = split(flat)
        both = jnp.concatenate([high, low], axis=0)
        out = lax.dot_general(both, both, NT, preferred_element_type=F32)
        cross = out[0:32, 32:64] + out[32:64, 0:32]
        gram[b, :, 0:32] = cross + out[0:32, 0:32]
        return 0

    lax.fori_loop(0, VISITS, gram_of, 0)

    lane = iota((LANES, LANES), 1)
    groups = []
    for g in range(4):
        picked = [gram[:, 8 * g + jj, :] for jj in range(8)]
        stacked = jnp.concatenate(picked, axis=0)
        groups.append(stacked.T[0:32])
    lane = iota((32, LANES), 1)
    sub = iota((32, LANES), 0)
    for g in range(4):
        diagonal = (sub == 8 * g + lane // VISITS) & (sub < columns)
        groups[g] = groups[g] + jnp.where(diagonal, RIDGE, 0.0)
    visit = lane % VISITS
    for k in range(columns):
        factor = jnp.take_along_axis(groups[k // 8], visit + VISITS * (k % 8), axis=1)
        pivot = factor[k : k + 1, :]
        inverse = 1.0 / pivot
        scaled = jnp.where(sub == k, (pivot - 1.0) * inverse, factor * inverse)
        for g in range(k // 8, 4):
            groups[g] = groups[g] - scaled * groups[g][k : k + 1, :]
    target = columns
    answer = jnp.take_along_axis(groups[target // 8], lane // SUBS + VISITS * (target % 8), axis=1)
    coeff = jnp.concatenate([answer, jnp.zeros((LANES - 32, LANES), F32)], axis=0).T

    residual = science - coeff[:, bases : bases + 1]
    for k in range(bases):
        residual = residual - coeff[:, k : k + 1] * design[k]
    out_ref[...] = residual.reshape(VISITS, SUBS, LANES)


def unpack_kernel(dest_ref, back_ref, out_ref, count):
    peers = back_ref.shape[0]
    strips = out_ref.shape[0]

    def clear(d, _):
        count[d] = 0
        return 0

    lax.fori_loop(0, peers, clear, 0, unroll=min(peers, 16))

    def pick(s, _):
        d = dest_ref[s, 0]
        rank = count[d]
        count[d] = rank + 1
        both = back_ref[d]
        half = SUBS // CAP
        out_ref[s] = jnp.where(rank == 0, both[0:half], both[half:SUBS])
        return 0

    lax.fori_loop(0, strips, pick, 0, unroll=min(strips, 16))


VMEM = pl.BlockSpec(memory_space=pltpu.VMEM)
SMEM = pl.BlockSpec(memory_space=pltpu.SMEM)
ANY = pl.BlockSpec(memory_space=pl.ANY)


def on_device(
    template, science, dest, row_offset, col_block, basis_rows, basis_cols, stamp_rows, stamp_cols
):
    peers = lax.axis_size("patch")
    own = lax.axis_index("patch").astype(jnp.int32)
    rows, cols = template.shape
    strips, strip_rows, block_cols = science.shape
    bases = basis_rows.shape[0]
    place = jnp.stack([own, jnp.int32(peers)])
    last = cols // LANES - 1

    payload = pl.pallas_call(
        pack_kernel,
        grid=(1,),
        out_shape=jax.ShapeDtypeStruct((peers, 2 * SUBS, LANES), F32),
        in_specs=[
            SMEM, SMEM, SMEM, SMEM,
            pl.BlockSpec((rows, LANES), lambda i: (0, 0)),
            pl.BlockSpec((rows, LANES), lambda i: (0, last)),
            VMEM,
        ],
        out_specs=VMEM,
        scratch_shapes=[pltpu.SMEM((peers,), jnp.int32), pltpu.SMEM((CAP * peers,), jnp.int32)],
        name="pack",
    )(place, dest, row_offset, col_block, template, template, science)

    arrived = lax.all_to_all(payload, "patch", split_axis=0, concat_axis=0, tiled=True)

    col_taps, row_taps, mask = pl.pallas_call(
        prep_kernel,
        out_shape=(
            jax.ShapeDtypeStruct((bases, 2 * LANES, 2 * LANES), BF16),
            jax.ShapeDtypeStruct((bases * SUBS, 2 * LANES), F32),
            jax.ShapeDtypeStruct((cols // LANES, rows + SUBS, LANES), F32),
        ),
        in_specs=[SMEM, VMEM, VMEM, VMEM, VMEM],
        out_specs=(VMEM, VMEM, VMEM),
        scratch_shapes=[pltpu.VMEM((32, LANES), F32), pltpu.VMEM((32, LANES), F32)],
        name="prep",
    )(place, basis_rows, basis_cols, stamp_rows, stamp_cols)

    per = VISITS * SUBS
    residual = pl.pallas_call(
        main_kernel,
        grid_spec=pltpu.PrefetchScalarGridSpec(
            num_scalar_prefetch=1,
            grid=(peers // VISITS,),
            in_specs=[
                pl.BlockSpec((VISITS, 2 * SUBS, LANES), lambda i, at: (i, 0, 0)),
                pl.BlockSpec((1, SUBS, LANES), lambda i, at: (jnp.maximum(at[0] - 1, 0), 1, 0)),
                pl.BlockSpec((1, SUBS, LANES), lambda i, at: (jnp.minimum(at[0] + 1, at[1] - 1), 1, 0)),
                pl.BlockSpec((rows, cols), lambda i, at: (0, 0)),
                ANY,
                pl.BlockSpec((bases * SUBS, 2 * LANES), lambda i, at: (0, 0)),
                pl.BlockSpec((cols // LANES, rows + SUBS, LANES), lambda i, at: (0, 0, 0)),
            ],
            out_specs=pl.BlockSpec((VISITS, SUBS, LANES), lambda i, at: (i, 0, 0)),
            scratch_shapes=[
                pltpu.VMEM((cols // LANES + 1, rows + 40, LANES), F32),
                pltpu.VMEM((VISITS, LANES), F32),
                pltpu.SMEM((VISITS, LANES), F32),
                pltpu.VMEM((bases, 2 * LANES, 2 * LANES), BF16),
                pltpu.VMEM((per, LANES), F32),
                pltpu.VMEM((bases, 2 * per, 2 * LANES), BF16),
                pltpu.VMEM((bases + 1, per, LANES), F32),
                pltpu.VMEM((32, per, LANES), F32),
                pltpu.VMEM((VISITS, 32, LANES), F32),
                pltpu.SemaphoreType.DMA,
                pltpu.SemaphoreType.DMA,
            ],
        ),
        out_shape=jax.ShapeDtypeStruct((peers, SUBS, LANES), F32),
        name="fit",
    )(place, arrived, arrived, arrived, template, col_taps, row_taps, mask)

    returned = lax.all_to_all(residual, "patch", split_axis=0, concat_axis=0, tiled=True)

    return pl.pallas_call(
        unpack_kernel,
        out_shape=jax.ShapeDtypeStruct(science.shape, F32),
        in_specs=[SMEM, VMEM],
        out_specs=VMEM,
        scratch_shapes=[pltpu.SMEM((peers,), jnp.int32)],
        name="unpack",
    )(dest, returned)


def solution(mesh):
    placed = (
        P(None, ("groups", "patch")),
        P(("groups", "patch"), None, None),
        P(("groups", "patch"), None),
        P(("groups", "patch")),
        P(("groups", "patch")),
        P(),
        P(),
        P("groups", None),
        P("groups", None),
    )
    return jax.shard_map(
        on_device,
        mesh=mesh,
        in_specs=placed,
        out_specs=P(("groups", "patch"), None, None),
        check_vma=False,
    )
```

```python
import jax
import jax.numpy as jnp
from jax import lax
from jax.experimental import pallas as pl
from jax.experimental.pallas import tpu as pltpu
from jax.sharding import PartitionSpec as P

CAP = 2
STAMP_HALF = 10
RIDGE = 1.0
LANES = 128
SUBS = 8
VISITS = 16
PITCH = VISITS * SUBS + 8

F32 = jnp.float32
BF16 = jnp.bfloat16
NT = (((1,), (1,)), ((), ()))


def iota(shape, dim):
    return lax.broadcasted_iota(jnp.int32, shape, dim)


def split(x):
    high = x.astype(BF16)
    return high, (x - high.astype(F32)).astype(BF16)


INFO_ROW = 2
SHIFT = 10
TOP = 16


def pack_kernel(dest_ref, row_ref, col_ref, first_ref, last_ref, science_ref, out_ref, count, source):
    peers = out_ref.shape[0]
    strips = science_ref.shape[0]
    own = lax.axis_index("patch")

    def clear(d, _):
        count[d] = 0
        for r in range(CAP):
            source[CAP * d + r] = -1
        return 0

    lax.fori_loop(0, peers, clear, 0, unroll=min(peers, 16))

    def place(s, _):
        d = dest_ref[s]
        rank = count[d]
        source[CAP * d + rank] = s
        count[d] = rank + 1
        return 0

    lax.fori_loop(0, strips, place, 0, unroll=min(strips, 16))

    edges = jnp.concatenate([first_ref[...], last_ref[...]], axis=0).T
    lane = iota((SUBS, LANES), 1)
    sub = iota((SUBS, LANES), 0)
    rows = LANES // 2
    low = lane < rows
    head = jnp.where(low, edges[0:8], pltpu.roll(edges[8:16], rows, 1))
    tail = jnp.where(low, pltpu.roll(edges[120:128], rows, 1), edges[112:120])
    info_here = (~low) & (sub == INFO_ROW)

    def fill(d, _):
        halo = jnp.where(d == own + 1, tail, head)
        info = jnp.zeros((SUBS, LANES), F32)
        parts = []
        for r in range(CAP):
            s = source[CAP * d + r]
            live = s >= 0
            at = jnp.maximum(s, 0)
            strip = science_ref[at]
            parts.append(jnp.where(live, strip, 0.0))
            values = (row_ref[at], col_ref[at], jnp.int32(1))
            for j, value in enumerate(values):
                value = jnp.where(live, value, 0).astype(F32)
                info = jnp.where(lane == rows + 3 * r + j, value, info)
        out_ref[d, 0:SUBS, :] = jnp.concatenate(parts, axis=0)
        out_ref[d, SUBS : 2 * SUBS, :] = jnp.where(info_here, info, halo)
        return 0

    lax.fori_loop(0, peers, fill, 0, unroll=min(peers, 16))


def prep_kernel(
    template_ref, rows_ref, cols_ref, stamp_r_ref, stamp_c_ref, frame_ref, col_taps_ref, row_taps_ref, mask_ref, pad_c, pad_t
):
    taps, bases = rows_ref.shape
    own = lax.axis_index("patch")
    rows = template_ref.shape[0]
    blocks = frame_ref.shape[0]
    frame_ref[:, 0:TOP, :] = jnp.zeros((blocks, TOP, LANES), F32)
    frame_ref[:, TOP + rows :, :] = jnp.zeros((blocks, frame_ref.shape[1] - TOP - rows, LANES), F32)
    starts = iota((rows, LANES), 1) < SHIFT
    before = jnp.zeros((rows, LANES), F32)
    for c in range(blocks):
        here = jnp.zeros((rows, LANES), F32)
        if c < blocks - 1:
            here = pltpu.roll(template_ref[:, LANES * c : LANES * (c + 1)], SHIFT, 1)
        frame_ref[c, TOP : TOP + rows, :] = jnp.where(starts, before, here)
        before = here
    blocks, sub_rows, _ = mask_ref.shape
    sub_rows = sub_rows - SUBS
    sub_cols = blocks * LANES
    centre_r = stamp_r_ref[pl.ds(own, 1), :]
    centre_c = stamp_c_ref[pl.ds(own, 1), :]
    stamps = centre_r.shape[1]
    row_hit = (jnp.abs(iota((sub_rows, stamps), 0) - centre_r) <= STAMP_HALF).astype(F32).astype(BF16)
    col_hit = (jnp.abs(iota((sub_cols, stamps), 0) - centre_c) <= STAMP_HALF).astype(F32).astype(BF16)
    counts = lax.dot_general(row_hit, col_hit, NT, preferred_element_type=F32)
    for c in range(blocks):
        mask_ref[c, 0:sub_rows, :] = jnp.minimum(counts[:, LANES * c : LANES * (c + 1)], 1.0)
        mask_ref[c, sub_rows:, :] = jnp.zeros((SUBS, LANES), F32)
    pad_t[...] = jnp.zeros_like(pad_t)
    pad_t[0:taps, 0:bases] = cols_ref[...]
    pad_t[32 : 32 + taps, 0:bases] = rows_ref[...]
    filters = pad_t[...].T
    pad_c[...] = jnp.where(iota((32, LANES), 1) < 32, filters[0:32], 0.0)
    full = jnp.where(iota((32, LANES), 1) < 32, pltpu.roll(filters[0:32], LANES - 32, 1), 0.0)
    high = full.astype(BF16).astype(F32)
    base = high + pltpu.roll(high, 32, 1) + pltpu.roll(full - high, 64, 1)
    wide = jnp.concatenate([base, jnp.zeros_like(base)], axis=1)
    lower = iota((SUBS, 2 * LANES), 0) < SUBS // CAP
    tiles = []
    for k in range(bases):
        row = jnp.broadcast_to(wide[k : k + 1, :], (SUBS, 2 * LANES))
        row = pltpu.roll(row, 0, 1, stride=1, stride_axis=0)
        row = jnp.where(lower, row, pltpu.roll(row, 96 - SUBS // CAP, 1))
        tiles.append(row)
    row_taps_ref[...] = jnp.concatenate(tiles, axis=0).astype(BF16)
    def column(k, _):
        ring = jnp.broadcast_to(pad_c[pl.ds(k, 1), :], (LANES, LANES))
        high, low = split(pltpu.roll(ring, 0, 1, stride=1, stride_axis=0))
        col_taps_ref[k, 0:LANES, :] = high
        col_taps_ref[k, LANES : 2 * LANES, :] = low
        return 0

    lax.fori_loop(0, bases, column, 0, unroll=9)


def main_kernel(
    arrived_ref, frame_ref, col_taps_ref, row_taps_ref, mask_ref, out_ref,
    frame, info_v, info_s, weight, field, design, weighted, gram, info_sem,
):
    own = lax.axis_index("patch")
    peers = arrived_ref.shape[0]
    bases = col_taps_ref.shape[0]
    rows = LANES // 2
    last = frame.shape[0] - 1
    per = VISITS * SUBS

    info_v[...] = arrived_ref[:, SUBS + INFO_ROW, :]
    info_copy = pltpu.make_async_copy(info_v, info_s, info_sem)
    info_copy.start()

    left = jnp.where(own > 0, arrived_ref[jnp.maximum(own - 1, 0), SUBS : 2 * SUBS, :], 0.0)
    right = jnp.where(own < peers - 1, arrived_ref[jnp.minimum(own + 1, peers - 1), SUBS : 2 * SUBS, :], 0.0)
    gap = jnp.zeros((LANES - 4 * SUBS, LANES), F32)
    halo = jnp.concatenate([pltpu.roll(right, 64, 1), right, gap, pltpu.roll(left, 64, 1), left], axis=0).T
    halo = pltpu.roll(halo, SHIFT, 1)
    starts = iota((rows, LANES), 1) < SHIFT
    frame[...] = frame_ref[...]
    frame[0, TOP : TOP + rows, :] = jnp.where(starts, halo[0:rows], frame_ref[0, TOP : TOP + rows, :])
    frame[last, TOP : TOP + rows, :] = jnp.where(starts, frame_ref[last, TOP : TOP + rows, :], halo[rows : 2 * rows])
    columns = bases + 1
    design[bases, :, :] = jnp.ones((per, LANES), F32)
    weighted[PITCH * (columns + 1) :, :] = jnp.zeros((weighted.shape[0] - PITCH * (columns + 1), LANES), F32)
    info_copy.wait()

    def fit_group(group, _):
        fit_visits(
            group, arrived_ref, col_taps_ref, row_taps_ref, mask_ref, out_ref,
            frame, info_s, weight, field, design, weighted, gram,
        )
        return 0

    if peers == VISITS:
        fit_group(0, 0)
    else:
        lax.fori_loop(0, peers // VISITS, fit_group, 0)


def fit_visits(
    group, arrived_ref, col_taps_ref, row_taps_ref, mask_ref, out_ref,
    frame, info_s, weight, field, design, weighted, gram,
):
    bases = col_taps_ref.shape[0]
    columns = bases + 1
    per = VISITS * SUBS
    row_taps = row_taps_ref[:, 0:192]

    def convolve_rows(pair, _):
        outs = []
        for half in range(2):
            b = 2 * pair + half
            visit = group * VISITS + b
            terms = []
            masks = []
            for r in range(CAP):
                first = info_s[visit, 64 + 3 * r].astype(jnp.int32)
                block = info_s[visit, 65 + 3 * r].astype(jnp.int32)
                live = info_s[visit, 66 + 3 * r]
                sides = [frame[block + side, pl.ds(first + 6, 32), :] for side in range(2)]
                window = jnp.concatenate(sides, axis=1)
                high, low = split(window)
                terms += [high, low, high]
                masks.append(mask_ref[block, pl.ds(first, SUBS), :][0 : SUBS // CAP] * live)
            weight[pl.ds(pl.multiple_of(SUBS * b, SUBS), SUBS), :] = jnp.concatenate(masks, axis=0)
            tall = jnp.concatenate(terms, axis=0)
            across = lax.dot_general(row_taps, tall, (((1,), (0,)), ((), ())), preferred_element_type=F32)
            outs.append(across.reshape(bases, SUBS, 2 * LANES))
        both = jnp.concatenate(outs, axis=1)
        high, low = split(both)
        at = pl.multiple_of(2 * SUBS * pair, 2 * SUBS)
        field[:, pl.ds(at, 2 * SUBS), :] = high
        field[:, pl.ds(per + at, 2 * SUBS), :] = low
        return 0

    lax.fori_loop(0, VISITS // 2, convolve_rows, 0, unroll=2)

    hits = weight[...]

    inside = iota((2 * LANES, LANES), 1) >= iota((2 * LANES, LANES), 0) % LANES

    def convolve_cols(k, _):
        ring = col_taps_ref[k]
        none = jnp.zeros_like(ring)
        band = jnp.concatenate([jnp.where(inside, ring, none), jnp.where(inside, none, ring)], axis=1)
        out = lax.dot_general(field[k], band, NT, preferred_element_type=F32)
        conv = (out[0:per, LANES:] + out[per:, 0:LANES]) + out[0:per, 0:LANES]
        design[k] = conv
        weighted[pl.ds(PITCH * k, per), :] = conv * hits
        return 0

    lax.fori_loop(0, bases, convolve_cols, 0, unroll=9)
    science = arrived_ref[pl.ds(group * VISITS, VISITS), 0:SUBS, :].reshape(per, LANES)
    weighted[PITCH * bases : PITCH * bases + per, :] = hits
    weighted[PITCH * columns : PITCH * columns + per, :] = science * hits

    def gram_of(b, _):
        flat = jnp.concatenate([weighted[pl.ds(SUBS * b + q, 32, stride=PITCH), :] for q in range(SUBS)], axis=1)
        high, low = split(flat)
        both = jnp.concatenate([high, low], axis=0)
        out = lax.dot_general(both, both, NT, preferred_element_type=F32)
        cross = out[0:32, 32:64] + out[32:64, 0:32]
        gram[b, :, 0:32] = cross + out[0:32, 0:32]
        return 0

    lax.fori_loop(0, VISITS, gram_of, 0, unroll=4)

    lane = iota((LANES, LANES), 1)
    groups = []
    for g in range(4):
        picked = [gram[:, 8 * g + jj, :] for jj in range(8)]
        stacked = jnp.concatenate(picked, axis=0)
        groups.append(stacked.T[0:32])
    lane = iota((32, LANES), 1)
    sub = iota((32, LANES), 0)
    for g in range(4):
        diagonal = (sub == 8 * g + lane // VISITS) & (sub < columns)
        groups[g] = groups[g] + jnp.where(diagonal, RIDGE, 0.0)
    visit = lane % VISITS
    for k in range(columns):
        factor = jnp.take_along_axis(groups[k // 8], visit + VISITS * (k % 8), axis=1)
        pivot = factor[k : k + 1, :]
        inverse = 1.0 / pivot
        scaled = jnp.where(sub == k, (pivot - 1.0) * inverse, factor * inverse)
        for g in range(k // 8, 4):
            groups[g] = groups[g] - scaled * groups[g][k : k + 1, :]
    target = columns
    answer = jnp.take_along_axis(groups[target // 8], lane // SUBS + VISITS * (target % 8), axis=1)
    coeff = jnp.concatenate([answer, jnp.zeros((LANES - 32, LANES), F32)], axis=0).T

    residual = science - coeff[:, bases : bases + 1]
    for k in range(bases):
        residual = residual - coeff[:, k : k + 1] * design[k]
    out_ref[pl.ds(group * VISITS, VISITS)] = residual.reshape(VISITS, SUBS, LANES)


def unpack_kernel(dest_ref, back_ref, out_ref, count):
    peers = back_ref.shape[0]
    strips = out_ref.shape[0]

    def clear(d, _):
        count[d] = 0
        return 0

    lax.fori_loop(0, peers, clear, 0, unroll=min(peers, 16))

    def pick(s, _):
        d = dest_ref[s]
        rank = count[d]
        count[d] = rank + 1
        both = back_ref[d]
        half = SUBS // CAP
        out_ref[s] = jnp.where(rank == 0, both[0:half], both[half:SUBS])
        return 0

    lax.fori_loop(0, strips, pick, 0, unroll=min(strips, 16))


VMEM = pl.BlockSpec(memory_space=pltpu.VMEM)
SMEM = pl.BlockSpec(memory_space=pltpu.SMEM)
HBM = pl.BlockSpec(memory_space=pltpu.HBM)


def on_device(
    template, science, dest, row_offset, col_block, basis_rows, basis_cols, stamp_rows, stamp_cols
):
    peers = lax.axis_size("patch")
    rows, cols = template.shape
    strips, strip_rows, block_cols = science.shape
    bases = basis_rows.shape[0]
    targets = dest.reshape(strips)
    last = cols // LANES - 1

    payload = pl.pallas_call(
        pack_kernel,
        grid=(1,),
        out_shape=jax.ShapeDtypeStruct((peers, 2 * SUBS, LANES), F32),
        in_specs=[
            SMEM, SMEM, SMEM,
            pl.BlockSpec((rows, LANES), lambda i: (0, 0)),
            pl.BlockSpec((rows, LANES), lambda i: (0, last)),
            VMEM,
        ],
        out_specs=VMEM,
        scratch_shapes=[pltpu.SMEM((peers,), jnp.int32), pltpu.SMEM((CAP * peers,), jnp.int32)],
        name="pack",
    )(targets, row_offset, col_block, template, template, science)

    arrived = lax.all_to_all(payload, "patch", split_axis=0, concat_axis=0, tiled=True)

    frame, col_taps, row_taps, mask = pl.pallas_call(
        prep_kernel,
        out_shape=(
            pltpu.VMEM((cols // LANES + 1, rows + 40, LANES), F32),
            pltpu.VMEM((bases, 2 * LANES, LANES), BF16),
            pltpu.VMEM((bases * SUBS, 2 * LANES), BF16),
            pltpu.VMEM((cols // LANES, rows + SUBS, LANES), F32),
        ),
        in_specs=[VMEM, VMEM, VMEM, VMEM, VMEM],
        out_specs=(VMEM, VMEM, VMEM, VMEM),
        scratch_shapes=[pltpu.VMEM((32, LANES), F32), pltpu.VMEM((LANES, LANES), F32)],
        name="prep",
    )(template, basis_rows.T, basis_cols.T, stamp_rows, stamp_cols)

    per = VISITS * SUBS
    residual = pl.pallas_call(
        main_kernel,
        in_specs=[VMEM, VMEM, VMEM, VMEM, VMEM],
        out_specs=VMEM,
        scratch_shapes=[
            pltpu.VMEM((cols // LANES + 1, rows + 40, LANES), F32),
            pltpu.VMEM((peers, LANES), F32),
            pltpu.SMEM((peers, LANES), F32),
            pltpu.VMEM((per, LANES), F32),
            pltpu.VMEM((bases, 2 * per, 2 * LANES), BF16),
            pltpu.VMEM((bases + 1, per, LANES), F32),
            pltpu.VMEM((32 * PITCH, LANES), F32),
            pltpu.VMEM((VISITS, 32, LANES), F32),
            pltpu.SemaphoreType.DMA,
        ],
        out_shape=jax.ShapeDtypeStruct((peers, SUBS, LANES), F32),
        compiler_params=pltpu.CompilerParams(vmem_limit_bytes=24 << 20),
        name="fit",
    )(arrived, frame, col_taps, row_taps, mask)

    returned = lax.all_to_all(residual, "patch", split_axis=0, concat_axis=0, tiled=True)

    return pl.pallas_call(
        unpack_kernel,
        out_shape=jax.ShapeDtypeStruct(science.shape, F32),
        in_specs=[SMEM, VMEM],
        out_specs=VMEM,
        scratch_shapes=[pltpu.SMEM((peers,), jnp.int32)],
        name="unpack",
    )(targets, returned)


def solution(mesh):
    placed = (
        P(None, ("groups", "patch")),
        P(("groups", "patch"), None, None),
        P(("groups", "patch"), None),
        P(("groups", "patch")),
        P(("groups", "patch")),
        P(),
        P(),
        P("groups", None),
        P("groups", None),
    )
    return jax.shard_map(
        on_device,
        mesh=mesh,
        in_specs=placed,
        out_specs=P(("groups", "patch"), None, None),
        check_vma=False,
    )
```

```python
import jax
import jax.numpy as jnp
from jax import lax
from jax.experimental import pallas as pl
from jax.experimental.pallas import tpu as pltpu
from jax.sharding import PartitionSpec as P

CAP = 2
STAMP_HALF = 10
RIDGE = 1.0
LANES = 128
SUBS = 8
VISITS = 16
PITCH = VISITS * SUBS + 8

F32 = jnp.float32
BF16 = jnp.bfloat16
NT = (((1,), (1,)), ((), ()))


def iota(shape, dim):
    return lax.broadcasted_iota(jnp.int32, shape, dim)


def split(x):
    high = x.astype(BF16)
    return high, (x - high.astype(F32)).astype(BF16)


INFO_ROW = 2
SHIFT = 10
TOP = 16


def pack_kernel(dest_ref, row_ref, col_ref, first_ref, last_ref, science_ref, out_ref, count, source):
    peers = out_ref.shape[0]
    strips = science_ref.shape[0]
    own = lax.axis_index("patch")

    def clear(d, _):
        count[d] = 0
        for r in range(CAP):
            source[CAP * d + r] = -1
        return 0

    lax.fori_loop(0, peers, clear, 0, unroll=min(peers, 16))

    def place(s, _):
        d = dest_ref[s]
        rank = count[d]
        source[CAP * d + rank] = s
        count[d] = rank + 1
        return 0

    lax.fori_loop(0, strips, place, 0, unroll=min(strips, 16))

    edges = jnp.concatenate([first_ref[...], last_ref[...]], axis=0).T
    lane = iota((SUBS, LANES), 1)
    sub = iota((SUBS, LANES), 0)
    rows = LANES // 2
    low = lane < rows
    head = jnp.where(low, edges[0:8], pltpu.roll(edges[8:16], rows, 1))
    tail = jnp.where(low, pltpu.roll(edges[120:128], rows, 1), edges[112:120])
    info_here = (~low) & (sub == INFO_ROW)

    def fill(d, _):
        halo = jnp.where(d == own + 1, tail, head)
        info = jnp.zeros((SUBS, LANES), F32)
        parts = []
        for r in range(CAP):
            s = source[CAP * d + r]
            live = s >= 0
            at = jnp.maximum(s, 0)
            strip = science_ref[at]
            parts.append(jnp.where(live, strip, 0.0))
            values = (row_ref[at], col_ref[at], jnp.int32(1))
            for j, value in enumerate(values):
                value = jnp.where(live, value, 0).astype(F32)
                info = jnp.where(lane == rows + 3 * r + j, value, info)
        out_ref[d, 0:SUBS, :] = jnp.concatenate(parts, axis=0)
        out_ref[d, SUBS : 2 * SUBS, :] = jnp.where(info_here, info, halo)
        return 0

    lax.fori_loop(0, peers, fill, 0, unroll=min(peers, 16))


def prep_kernel(
    template_ref, rows_ref, cols_ref, stamp_r_ref, stamp_c_ref, frame_ref, col_taps_ref, row_taps_ref, mask_ref, pad_c, pad_t
):
    taps, bases = rows_ref.shape
    own = lax.axis_index("patch")
    rows = template_ref.shape[0]
    blocks = frame_ref.shape[0]
    frame_ref[:, 0:TOP, :] = jnp.zeros((blocks, TOP, LANES), F32)
    frame_ref[:, TOP + rows :, :] = jnp.zeros((blocks, frame_ref.shape[1] - TOP - rows, LANES), F32)
    starts = iota((rows, LANES), 1) < SHIFT
    before = jnp.zeros((rows, LANES), F32)
    for c in range(blocks):
        here = jnp.zeros((rows, LANES), F32)
        if c < blocks - 1:
            here = pltpu.roll(template_ref[:, LANES * c : LANES * (c + 1)], SHIFT, 1)
        frame_ref[c, TOP : TOP + rows, :] = jnp.where(starts, before, here)
        before = here
    blocks, sub_rows, _ = mask_ref.shape
    sub_rows = sub_rows - SUBS
    sub_cols = blocks * LANES
    centre_r = stamp_r_ref[pl.ds(own, 1), :]
    centre_c = stamp_c_ref[pl.ds(own, 1), :]
    stamps = centre_r.shape[1]
    row_hit = (jnp.abs(iota((sub_rows, stamps), 0) - centre_r) <= STAMP_HALF).astype(F32).astype(BF16)
    col_hit = (jnp.abs(iota((sub_cols, stamps), 0) - centre_c) <= STAMP_HALF).astype(F32).astype(BF16)
    counts = lax.dot_general(row_hit, col_hit, NT, preferred_element_type=F32)
    for c in range(blocks):
        mask_ref[c, 0:sub_rows, :] = jnp.minimum(counts[:, LANES * c : LANES * (c + 1)], 1.0)
        mask_ref[c, sub_rows:, :] = jnp.zeros((SUBS, LANES), F32)
    pad_t[...] = jnp.zeros_like(pad_t)
    pad_t[0:taps, 0:bases] = cols_ref[...]
    pad_t[32 : 32 + taps, 0:bases] = rows_ref[...]
    filters = pad_t[...].T
    pad_c[...] = jnp.where(iota((32, LANES), 1) < 32, filters[0:32], 0.0)
    full = jnp.where(iota((32, LANES), 1) < 32, pltpu.roll(filters[0:32], LANES - 32, 1), 0.0)
    high = full.astype(BF16).astype(F32)
    base = high + pltpu.roll(high, 32, 1) + pltpu.roll(full - high, 64, 1)
    wide = jnp.concatenate([base, jnp.zeros_like(base)], axis=1)
    lower = iota((SUBS, 2 * LANES), 0) < SUBS // CAP
    tiles = []
    for k in range(bases):
        row = jnp.broadcast_to(wide[k : k + 1, :], (SUBS, 2 * LANES))
        row = pltpu.roll(row, 0, 1, stride=1, stride_axis=0)
        row = jnp.where(lower, row, pltpu.roll(row, 96 - SUBS // CAP, 1))
        tiles.append(row)
    row_taps_ref[...] = jnp.concatenate(tiles, axis=0).astype(BF16)
    def column(k, _):
        ring = jnp.broadcast_to(pad_c[pl.ds(k, 1), :], (LANES, LANES))
        high, low = split(pltpu.roll(ring, 0, 1, stride=1, stride_axis=0))
        col_taps_ref[k, 0:LANES, :] = high
        col_taps_ref[k, LANES : 2 * LANES, :] = low
        return 0

    lax.fori_loop(0, bases, column, 0, unroll=9)


def main_kernel(
    arrived_ref, frame_ref, col_taps_ref, row_taps_ref, mask_ref, out_ref,
    frame, info_v, info_s, weight, field, design, weighted, gram, info_sem,
):
    own = lax.axis_index("patch")
    peers = arrived_ref.shape[0]
    bases = col_taps_ref.shape[0]
    rows = LANES // 2
    last = frame.shape[0] - 1
    per = VISITS * SUBS

    info_v[...] = arrived_ref[:, SUBS + INFO_ROW, :]
    info_copy = pltpu.make_async_copy(info_v, info_s, info_sem)
    info_copy.start()

    left = jnp.where(own > 0, arrived_ref[jnp.maximum(own - 1, 0), SUBS : 2 * SUBS, :], 0.0)
    right = jnp.where(own < peers - 1, arrived_ref[jnp.minimum(own + 1, peers - 1), SUBS : 2 * SUBS, :], 0.0)
    gap = jnp.zeros((LANES - 4 * SUBS, LANES), F32)
    halo = jnp.concatenate([pltpu.roll(right, 64, 1), right, gap, pltpu.roll(left, 64, 1), left], axis=0).T
    halo = pltpu.roll(halo, SHIFT, 1)
    starts = iota((rows, LANES), 1) < SHIFT
    frame[...] = frame_ref[...]
    frame[0, TOP : TOP + rows, :] = jnp.where(starts, halo[0:rows], frame_ref[0, TOP : TOP + rows, :])
    frame[last, TOP : TOP + rows, :] = jnp.where(starts, frame_ref[last, TOP : TOP + rows, :], halo[rows : 2 * rows])
    columns = bases + 1
    design[bases, :, :] = jnp.ones((per, LANES), F32)
    weighted[PITCH * (columns + 1) :, :] = jnp.zeros((weighted.shape[0] - PITCH * (columns + 1), LANES), F32)
    info_copy.wait()

    def fit_group(group, _):
        fit_visits(
            group, arrived_ref, col_taps_ref, row_taps_ref, mask_ref, out_ref,
            frame, info_s, weight, field, design, weighted, gram,
        )
        return 0

    if peers == VISITS:
        fit_group(0, 0)
    else:
        lax.fori_loop(0, peers // VISITS, fit_group, 0)


def fit_visits(
    group, arrived_ref, col_taps_ref, row_taps_ref, mask_ref, out_ref,
    frame, info_s, weight, field, design, weighted, gram,
):
    bases = col_taps_ref.shape[0]
    columns = bases + 1
    per = VISITS * SUBS
    row_taps = row_taps_ref[:, 0:192]

    def convolve_rows(pair, _):
        outs = []
        for half in range(2):
            b = 2 * pair + half
            visit = group * VISITS + b
            terms = []
            masks = []
            for r in range(CAP):
                first = info_s[visit, 64 + 3 * r].astype(jnp.int32)
                block = info_s[visit, 65 + 3 * r].astype(jnp.int32)
                live = info_s[visit, 66 + 3 * r]
                sides = [frame[block + side, pl.ds(first + 6, 32), :] for side in range(2)]
                window = jnp.concatenate(sides, axis=1)
                high, low = split(window)
                terms += [high, low, high]
                masks.append(mask_ref[block, pl.ds(first, SUBS), :][0 : SUBS // CAP] * live)
            weight[pl.ds(pl.multiple_of(SUBS * b, SUBS), SUBS), :] = jnp.concatenate(masks, axis=0)
            tall = jnp.concatenate(terms, axis=0)
            across = lax.dot_general(row_taps, tall, (((1,), (0,)), ((), ())), preferred_element_type=F32)
            outs.append(across.reshape(bases, SUBS, 2 * LANES))
        both = jnp.concatenate(outs, axis=1)
        high, low = split(both)
        at = pl.multiple_of(2 * SUBS * pair, 2 * SUBS)
        field[:, pl.ds(at, 2 * SUBS), :] = high
        field[:, pl.ds(per + at, 2 * SUBS), :] = low
        return 0

    lax.fori_loop(0, VISITS // 2, convolve_rows, 0, unroll=VISITS // 2)

    hits = weight[...]

    inside = iota((2 * LANES, LANES), 1) >= iota((2 * LANES, LANES), 0) % LANES

    def convolve_cols(k, _):
        ring = col_taps_ref[k]
        none = jnp.zeros_like(ring)
        band = jnp.concatenate([jnp.where(inside, ring, none), jnp.where(inside, none, ring)], axis=1)
        out = lax.dot_general(field[k], band, NT, preferred_element_type=F32)
        conv = (out[0:per, LANES:] + out[per:, 0:LANES]) + out[0:per, 0:LANES]
        design[k] = conv
        weighted[pl.ds(PITCH * k, per), :] = conv * hits
        return 0

    lax.fori_loop(0, bases, convolve_cols, 0, unroll=bases)
    science = arrived_ref[pl.ds(group * VISITS, VISITS), 0:SUBS, :].reshape(per, LANES)
    weighted[PITCH * bases : PITCH * bases + per, :] = hits
    weighted[PITCH * columns : PITCH * columns + per, :] = science * hits

    def gram_of(b, _):
        flat = jnp.concatenate([weighted[pl.ds(SUBS * b + q, 32, stride=PITCH), :] for q in range(SUBS)], axis=1)
        high, low = split(flat)
        both = jnp.concatenate([high, low], axis=0)
        out = lax.dot_general(both, both, NT, preferred_element_type=F32)
        cross = out[0:32, 32:64] + out[32:64, 0:32]
        gram[b, :, 0:32] = (out[32:64, 32:64] + cross) + out[0:32, 0:32]
        return 0

    lax.fori_loop(0, VISITS, gram_of, 0, unroll=8)

    lane = iota((LANES, LANES), 1)
    groups = []
    for g in range(4):
        picked = [gram[:, 8 * g + jj, :] for jj in range(8)]
        stacked = jnp.concatenate(picked, axis=0)
        groups.append(stacked.T[0:32])
    lane = iota((32, LANES), 1)
    sub = iota((32, LANES), 0)
    for g in range(4):
        diagonal = (sub == 8 * g + lane // VISITS) & (sub < columns)
        groups[g] = groups[g] + jnp.where(diagonal, RIDGE, 0.0)
    visit = lane % VISITS
    scale = jnp.zeros((32, LANES), F32)
    for p in range(4):
        ends = min(8 * p + 8, columns + 1)
        panel = {j: jnp.take_along_axis(groups[p], visit + VISITS * (j - 8 * p), axis=1) for j in range(8 * p, ends)}
        for k in range(8 * p, min(ends, columns)):
            here = sub == k
            inverse = 1.0 / panel[k][k : k + 1, :]
            scaled = jnp.where(here, 0.0, panel[k] * inverse)
            scale = jnp.where(here, inverse, scale)
            for j in range(k + 1, ends):
                panel[j] = panel[j] - scaled * panel[j][k : k + 1, :]
            for g in range(p + 1, 4):
                groups[g] = groups[g] - scaled * groups[g][k : k + 1, :]
    answer = panel[columns] * scale
    answer = jnp.take_along_axis(answer, lane // SUBS, axis=1)
    coeff = jnp.concatenate([answer, jnp.zeros((LANES - 32, LANES), F32)], axis=0).T

    residual = science - coeff[:, bases : bases + 1]
    for k in range(bases):
        residual = residual - coeff[:, k : k + 1] * design[k]
    out_ref[pl.ds(group * VISITS, VISITS)] = residual.reshape(VISITS, SUBS, LANES)


def unpack_kernel(dest_ref, back_ref, out_ref, count):
    peers = back_ref.shape[0]
    strips = out_ref.shape[0]

    def clear(d, _):
        count[d] = 0
        return 0

    lax.fori_loop(0, peers, clear, 0, unroll=min(peers, 16))

    def pick(s, _):
        d = dest_ref[s]
        rank = count[d]
        count[d] = rank + 1
        both = back_ref[d]
        half = SUBS // CAP
        out_ref[s] = jnp.where(rank == 0, both[0:half], both[half:SUBS])
        return 0

    lax.fori_loop(0, strips, pick, 0, unroll=min(strips, 16))


VMEM = pl.BlockSpec(memory_space=pltpu.VMEM)
SMEM = pl.BlockSpec(memory_space=pltpu.SMEM)
HBM = pl.BlockSpec(memory_space=pltpu.HBM)


def on_device(
    template, science, dest, row_offset, col_block, basis_rows, basis_cols, stamp_rows, stamp_cols
):
    peers = lax.axis_size("patch")
    rows, cols = template.shape
    strips, strip_rows, block_cols = science.shape
    bases = basis_rows.shape[0]
    targets = dest.reshape(strips)
    last = cols // LANES - 1

    payload = pl.pallas_call(
        pack_kernel,
        grid=(1,),
        out_shape=(pltpu.VMEM if peers <= VISITS else jax.ShapeDtypeStruct)((peers, 2 * SUBS, LANES), F32),
        in_specs=[
            SMEM, SMEM, SMEM,
            pl.BlockSpec((rows, LANES), lambda i: (0, 0)),
            pl.BlockSpec((rows, LANES), lambda i: (0, last)),
            VMEM,
        ],
        out_specs=VMEM,
        scratch_shapes=[pltpu.SMEM((peers,), jnp.int32), pltpu.SMEM((CAP * peers,), jnp.int32)],
        name="pack",
    )(targets, row_offset, col_block, template, template, science)

    arrived = lax.all_to_all(payload, "patch", split_axis=0, concat_axis=0, tiled=True)

    frame, col_taps, row_taps, mask = pl.pallas_call(
        prep_kernel,
        out_shape=(
            pltpu.VMEM((cols // LANES + 1, rows + 40, LANES), F32),
            pltpu.VMEM((bases, 2 * LANES, LANES), BF16),
            pltpu.VMEM((bases * SUBS, 2 * LANES), BF16),
            pltpu.VMEM((cols // LANES, rows + SUBS, LANES), F32),
        ),
        in_specs=[VMEM, VMEM, VMEM, VMEM, VMEM],
        out_specs=(VMEM, VMEM, VMEM, VMEM),
        scratch_shapes=[pltpu.VMEM((32, LANES), F32), pltpu.VMEM((LANES, LANES), F32)],
        name="prep",
    )(template, basis_rows.T, basis_cols.T, stamp_rows, stamp_cols)

    per = VISITS * SUBS
    residual = pl.pallas_call(
        main_kernel,
        in_specs=[VMEM, VMEM, VMEM, VMEM, VMEM],
        out_specs=VMEM,
        scratch_shapes=[
            pltpu.VMEM((cols // LANES + 1, rows + 40, LANES), F32),
            pltpu.VMEM((peers, LANES), F32),
            pltpu.SMEM((peers, LANES), F32),
            pltpu.VMEM((per, LANES), F32),
            pltpu.VMEM((bases, 2 * per, 2 * LANES), BF16),
            pltpu.VMEM((bases + 1, per, LANES), F32),
            pltpu.VMEM((32 * PITCH, LANES), F32),
            pltpu.VMEM((VISITS, 32, LANES), F32),
            pltpu.SemaphoreType.DMA,
        ],
        out_shape=jax.ShapeDtypeStruct((peers, SUBS, LANES), F32),
        compiler_params=pltpu.CompilerParams(vmem_limit_bytes=24 << 20),
        name="fit",
    )(arrived, frame, col_taps, row_taps, mask)

    returned = lax.all_to_all(residual, "patch", split_axis=0, concat_axis=0, tiled=True)

    return pl.pallas_call(
        unpack_kernel,
        out_shape=jax.ShapeDtypeStruct(science.shape, F32),
        in_specs=[SMEM, VMEM],
        out_specs=VMEM,
        scratch_shapes=[pltpu.SMEM((peers,), jnp.int32)],
        compiler_params=pltpu.CompilerParams(vmem_limit_bytes=8 << 20),
        name="unpack",
    )(targets, returned)


def solution(mesh):
    placed = (
        P(None, ("groups", "patch")),
        P(("groups", "patch"), None, None),
        P(("groups", "patch"), None),
        P(("groups", "patch")),
        P(("groups", "patch")),
        P(),
        P(),
        P("groups", None),
        P("groups", None),
    )
    return jax.shard_map(
        on_device,
        mesh=mesh,
        in_specs=placed,
        out_specs=P(("groups", "patch"), None, None),
        check_vma=False,
    )
```

```python
import jax
import jax.numpy as jnp
from jax import lax
from jax.experimental import pallas as pl
from jax.experimental.pallas import tpu as pltpu
from jax.sharding import PartitionSpec as P

CAP = 2
STAMP_HALF = 10
RIDGE = 1.0
LANES = 128
SUBS = 8
VISITS = 16
PITCH = VISITS * SUBS + 8

F32 = jnp.float32
BF16 = jnp.bfloat16
NT = (((1,), (1,)), ((), ()))


def iota(shape, dim):
    return lax.broadcasted_iota(jnp.int32, shape, dim)


def split(x):
    high = x.astype(BF16)
    return high, (x - high.astype(F32)).astype(BF16)


INFO_ROW = 2
SHIFT = 10
TOP = 16
HEIGHT = 40


def pack_kernel(
    dest_hbm, row_hbm, col_hbm, template_hbm, science_hbm, out_ref, slot_ref,
    dest_ref, row_ref, col_ref, edge, science_ref, count, source, sems,
):
    peers = out_ref.shape[0]
    strips = science_ref.shape[0]
    own = lax.axis_index("patch")
    rows = LANES // 2
    last = template_hbm.shape[1] - LANES
    copies = [
        pltpu.make_async_copy(source_ref, target_ref, sems.at[i])
        for i, (source_ref, target_ref) in enumerate(
            (
                (dest_hbm, dest_ref),
                (template_hbm.at[:, 0:LANES], edge.at[0:rows]),
                (template_hbm.at[:, last : last + LANES], edge.at[rows : 2 * rows]),
                (row_hbm, row_ref),
                (col_hbm, col_ref),
                (science_hbm, science_ref),
            )
        )
    ]
    for copy in copies:
        copy.start()

    def clear(d, _):
        count[d] = 0
        for r in range(CAP):
            source[CAP * d + r] = -1
        return 0

    lax.fori_loop(0, peers, clear, 0, unroll=min(peers, 16))

    def place(s, _):
        d = dest_ref[s]
        rank = count[d]
        source[CAP * d + rank] = s
        slot_ref[s] = CAP * d + rank
        count[d] = rank + 1
        return 0

    copies[0].wait()
    lax.fori_loop(0, strips, place, 0, unroll=min(strips, 16))
    for copy in copies[1:]:
        copy.wait()

    edges = edge[...].T
    lane = iota((SUBS, LANES), 1)
    sub = iota((SUBS, LANES), 0)
    low = lane < rows
    head = jnp.where(low, edges[0:8], pltpu.roll(edges[8:16], rows, 1))
    tail = jnp.where(low, pltpu.roll(edges[120:128], rows, 1), edges[112:120])
    info_here = (~low) & (sub == INFO_ROW)

    def fill(d, _):
        halo = jnp.where(d == own + 1, tail, head)
        info = jnp.zeros((SUBS, LANES), F32)
        parts = []
        for r in range(CAP):
            s = source[CAP * d + r]
            live = s >= 0
            at = jnp.maximum(s, 0)
            strip = science_ref[at]
            parts.append(jnp.where(live, strip, 0.0))
            values = (row_ref[at], col_ref[at], jnp.int32(1))
            for j, value in enumerate(values):
                value = jnp.where(live, value, 0).astype(F32)
                info = jnp.where(lane == rows + 3 * r + j, value, info)
        out_ref[d, 0:SUBS, :] = jnp.concatenate(parts, axis=0)
        out_ref[d, SUBS : 2 * SUBS, :] = jnp.where(info_here, info, halo)
        return 0

    lax.fori_loop(0, peers, fill, 0, unroll=min(peers, 16))


def prep_kernel(
    template_ref, rows_ref, cols_ref, stamp_r_ref, stamp_c_ref, frame_ref, col_taps_ref, row_taps_ref, mask_ref, pad_c, pad_t
):
    taps, bases = rows_ref.shape
    own = lax.axis_index("patch")
    rows = template_ref.shape[0]
    height = rows + HEIGHT
    blocks = frame_ref.shape[0] // height
    starts = iota((rows, LANES), 1) < SHIFT
    before = jnp.zeros((rows, LANES), F32)
    for c in range(blocks):
        here = jnp.zeros((rows, LANES), F32)
        if c < blocks - 1:
            here = pltpu.roll(template_ref[:, LANES * c : LANES * (c + 1)], SHIFT, 1)
        at = height * c
        frame_ref[at : at + TOP, :] = jnp.zeros((TOP, LANES), F32)
        frame_ref[at + TOP : at + TOP + rows, :] = jnp.where(starts, before, here)
        frame_ref[at + TOP + rows : at + height, :] = jnp.zeros((HEIGHT - TOP, LANES), F32)
        before = here
    sub_rows = rows
    blocks = blocks - 1
    sub_cols = blocks * LANES
    centre_r = stamp_r_ref[pl.ds(own, 1), :]
    centre_c = stamp_c_ref[pl.ds(own, 1), :]
    stamps = centre_r.shape[1]
    row_hit = (jnp.abs(iota((sub_rows, stamps), 0) - centre_r) <= STAMP_HALF).astype(F32).astype(BF16)
    col_hit = (jnp.abs(iota((sub_cols, stamps), 0) - centre_c) <= STAMP_HALF).astype(F32).astype(BF16)
    counts = lax.dot_general(row_hit, col_hit, NT, preferred_element_type=F32)
    for c in range(blocks):
        at = height * c
        mask_ref[at : at + height, :] = jnp.zeros((height, LANES), F32)
        mask_ref[at + TOP - SHIFT : at + TOP - SHIFT + rows, :] = jnp.minimum(counts[:, LANES * c : LANES * (c + 1)], 1.0)
    pad_t[...] = jnp.zeros_like(pad_t)
    pad_t[0:taps, 0:bases] = cols_ref[...]
    pad_t[32 : 32 + taps, 0:bases] = rows_ref[...]
    filters = pad_t[...].T
    pad_c[...] = jnp.where(iota((32, LANES), 1) < 32, filters[0:32], 0.0)
    full = jnp.where(iota((32, LANES), 1) < 32, pltpu.roll(filters[0:32], LANES - 32, 1), 0.0)
    high = full.astype(BF16).astype(F32)
    base = high + pltpu.roll(high, 32, 1) + pltpu.roll(full - high, 64, 1)
    wide = jnp.concatenate([base, jnp.zeros_like(base)], axis=1)
    lower = iota((SUBS, 2 * LANES), 0) < SUBS // CAP
    tiles = []
    for k in range(bases):
        row = jnp.broadcast_to(wide[k : k + 1, :], (SUBS, 2 * LANES))
        row = pltpu.roll(row, 0, 1, stride=1, stride_axis=0)
        row = jnp.where(lower, row, pltpu.roll(row, 96 - SUBS // CAP, 1))
        tiles.append(row)
    row_taps_ref[...] = jnp.concatenate(tiles, axis=0).astype(BF16)
    def column(k, _):
        ring = jnp.broadcast_to(pad_c[pl.ds(k, 1), :], (LANES, LANES))
        high, low = split(pltpu.roll(ring, 0, 1, stride=1, stride_axis=0))
        col_taps_ref[k, 0:LANES, :] = high
        col_taps_ref[k, LANES : 2 * LANES, :] = low
        return 0

    lax.fori_loop(0, bases, column, 0, unroll=9)


def main_kernel(
    arrived_ref, frame_ref, col_taps_ref, row_taps_ref, mask_ref, out_ref,
    frame, weight, field, design, pairs, gram,
):
    own = lax.axis_index("patch")
    peers = arrived_ref.shape[0]
    bases = col_taps_ref.shape[0]
    rows = LANES // 2
    last = frame.shape[0] - rows - HEIGHT
    per = VISITS * SUBS

    left = jnp.where(own > 0, arrived_ref[jnp.maximum(own - 1, 0), SUBS : 2 * SUBS, :], 0.0)
    right = jnp.where(own < peers - 1, arrived_ref[jnp.minimum(own + 1, peers - 1), SUBS : 2 * SUBS, :], 0.0)
    gap = jnp.zeros((LANES - 4 * SUBS, LANES), F32)
    halo = jnp.concatenate([pltpu.roll(right, 64, 1), right, gap, pltpu.roll(left, 64, 1), left], axis=0).T
    halo = pltpu.roll(halo, SHIFT, 1)
    starts = iota((rows, LANES), 1) < SHIFT
    frame[...] = frame_ref[...]
    first_rows = slice(TOP, TOP + rows)
    last_rows = slice(last + TOP, last + TOP + rows)
    frame[first_rows, :] = jnp.where(starts, halo[0:rows], frame_ref[first_rows, :])
    frame[last_rows, :] = jnp.where(starts, frame_ref[last_rows, :], halo[rows : 2 * rows])
    columns = bases + 1
    design[PITCH * bases : PITCH * bases + per, :] = jnp.ones((per, LANES), F32)
    design[PITCH * (columns + 1) :, :] = jnp.zeros((design.shape[0] - PITCH * (columns + 1), LANES), F32)

    def fit_group(group, _):
        fit_visits(
            group, arrived_ref, col_taps_ref, row_taps_ref, mask_ref, out_ref,
            frame, weight, field, design, pairs, gram,
        )
        return 0

    if peers == VISITS:
        fit_group(0, 0)
    else:
        lax.fori_loop(0, peers // VISITS, fit_group, 0)


def fit_visits(
    group, arrived_ref, col_taps_ref, row_taps_ref, mask_ref, out_ref,
    frame, weight, field, design, pairs, gram,
):
    bases = col_taps_ref.shape[0]
    columns = bases + 1
    per = VISITS * SUBS
    row_taps = row_taps_ref[:, 0:192]

    height = LANES // 2 + HEIGHT
    info = arrived_ref[pl.ds(group * VISITS, VISITS), SUBS + INFO_ROW, :]
    block = pltpu.roll(info, LANES - 1, 1)
    live = pltpu.roll(info, LANES - 2, 1)
    places = jnp.where(live > 0.0, block * height + info + (TOP - SHIFT), height - 32.0).astype(jnp.int32)

    for b in range(VISITS):
        terms = []
        masks = []
        for r in range(CAP):
            first = places[b, LANES // 2 + 3 * r]
            sides = [frame[pl.ds(first + height * side, 32), :] for side in range(2)]
            high, low = split(jnp.concatenate(sides, axis=1))
            terms += [high, low, high]
            masks.append(mask_ref[pl.ds(first, SUBS), :][0 : SUBS // CAP])
        at = slice(SUBS * b, SUBS * (b + 1))
        weight[at, :] = jnp.concatenate(masks, axis=0)
        across = jnp.dot(row_taps, jnp.concatenate(terms, axis=0), preferred_element_type=F32)
        for k in range(bases):
            field[k, at, :] = across[SUBS * k : SUBS * (k + 1)]

    turn = LANES - 32
    inside = iota((32, LANES), 1) >= iota((32, LANES), 0) + turn

    def convolve_cols(k, _):
        bands = []
        for term in range(2):
            ring = col_taps_ref[k, LANES * term : LANES * (term + 1), :]
            ends = ring[turn:]
            none = jnp.zeros_like(ends)
            here = jnp.concatenate([ring[0:turn], jnp.where(inside, ends, none)], axis=0)
            beyond = jnp.concatenate([jnp.zeros_like(ring[0:turn]), jnp.where(inside, none, ends)], axis=0)
            bands.append(jnp.concatenate([here, beyond], axis=1))
        both = jnp.concatenate(split(field[k]), axis=0)
        out = lax.dot_general(both, jnp.concatenate(bands, axis=0), NT, preferred_element_type=F32)
        conv = (out[0:per, LANES:] + out[per:, 0:LANES]) + out[0:per, 0:LANES]
        design[pl.ds(PITCH * k, per), :] = conv
        return 0

    lax.fori_loop(0, bases, convolve_cols, 0, unroll=bases)
    science = arrived_ref[pl.ds(group * VISITS, VISITS), 0:SUBS, :].reshape(per, LANES)
    design[PITCH * columns : PITCH * columns + per, :] = science

    def gram_of(b, _):
        left, right = [], []
        for q in range(SUBS):
            high, low = split(design[pl.ds(SUBS * b + q, 32, stride=PITCH), :])
            hit = jnp.broadcast_to(weight[pl.ds(SUBS * b + q, 1), :], (32, LANES)).astype(BF16)
            both = jnp.concatenate([high, low], axis=0)
            left.append(both * jnp.concatenate([hit, hit], axis=0))
            right.append(both)
            pairs[b, 32 * q : 32 * (q + 1), 0:LANES] = high
            pairs[b, 32 * q : 32 * (q + 1), LANES:] = low
        left = jnp.concatenate(left, axis=1)
        right = jnp.concatenate(right, axis=1)
        out = lax.dot_general(left, right, NT, preferred_element_type=F32)
        cross = out[0:32, 32:64] + out[32:64, 0:32]
        gram[b, :, 0:32] = (out[32:64, 32:64] + cross) + out[0:32, 0:32]
        return 0

    lax.fori_loop(0, VISITS, gram_of, 0, unroll=16)

    lane = iota((LANES, LANES), 1)
    groups = []
    for g in range(4):
        picked = [gram[:, 8 * g + jj, :] for jj in range(8)]
        stacked = jnp.concatenate(picked, axis=0)
        groups.append(stacked[:, 0:32].T)
    lane = iota((32, LANES), 1)
    sub = iota((32, LANES), 0)
    for g in range(4):
        diagonal = (sub == 8 * g + lane // VISITS) & (sub < columns)
        groups[g] = groups[g] + jnp.where(diagonal, RIDGE, 0.0)
    visit = lane % VISITS
    scale = jnp.zeros((32, LANES), F32)
    for p in range(4):
        ends = min(8 * p + 8, columns + 1)
        panel = {j: jnp.take_along_axis(groups[p], visit + VISITS * (j - 8 * p), axis=1) for j in range(8 * p, ends)}
        for k in range(8 * p, min(ends, columns)):
            here = sub == k
            inverse = 1.0 / panel[k][k : k + 1, :]
            scaled = jnp.where(here, 0.0, panel[k] * inverse)
            scale = jnp.where(here, inverse, scale)
            for j in range(k + 1, ends):
                panel[j] = panel[j] - scaled * panel[j][k : k + 1, :]
            for g in range(p + 1, 4):
                groups[g] = groups[g] - scaled * groups[g][k : k + 1, :]
    answer = panel[columns] * scale
    answer = jnp.take_along_axis(answer, lane // SUBS, axis=1)
    coeff = jnp.concatenate([answer, jnp.zeros((LANES - 32, LANES), F32)], axis=0).T

    tiled = coeff + pltpu.roll(coeff, 32, 1)
    tiled = tiled + pltpu.roll(tiled, 64, 1)
    row = iota((SUBS, LANES), 0)
    side = iota((SUBS, LANES), 1) // 32
    for b in range(VISITS):
        own_rows = tiled[SUBS * b : SUBS * (b + 1)]
        spread = jnp.concatenate([jnp.where(side == row, own_rows, 0.0), jnp.where(side + 4 == row, own_rows, 0.0)], axis=1)
        high = spread.astype(BF16).astype(F32)
        terms = jnp.concatenate([high, spread - high], axis=0).astype(BF16)
        out = lax.dot_general(terms, pairs[b], (((1,), (0,)), ((), ())), preferred_element_type=F32)
        model = (out[0:SUBS, LANES:] + out[SUBS:, 0:LANES]) + out[0:SUBS, 0:LANES]
        out_ref[group * VISITS + b] = science[SUBS * b : SUBS * (b + 1)] - model


def unpack_kernel(slot_ref, back_ref, out_ref):
    strips = out_ref.shape[0]
    half = SUBS // CAP

    def pick(s, _):
        slot = slot_ref[s]
        both = back_ref[slot // CAP]
        out_ref[s] = jnp.where(slot % CAP == 0, both[0:half], both[half:SUBS])
        return 0

    lax.fori_loop(0, strips, pick, 0, unroll=min(strips, 16))


VMEM = pl.BlockSpec(memory_space=pltpu.VMEM)
SMEM = pl.BlockSpec(memory_space=pltpu.SMEM)
ANY = pl.BlockSpec(memory_space=pl.ANY)


def on_device(
    template, science, dest, row_offset, col_block, basis_rows, basis_cols, stamp_rows, stamp_cols
):
    peers = lax.axis_size("patch")
    rows, cols = template.shape
    strips, strip_rows, block_cols = science.shape
    bases = basis_rows.shape[0]
    blocks = cols // LANES
    height = rows + HEIGHT
    targets = dest.reshape(strips)

    kept = pltpu.VMEM if peers <= VISITS else jax.ShapeDtypeStruct
    payload, slots = pl.pallas_call(
        pack_kernel,
        out_shape=(kept((peers, 2 * SUBS, LANES), F32), pltpu.SMEM((strips,), jnp.int32)),
        in_specs=[ANY, ANY, ANY, ANY, ANY],
        out_specs=(VMEM, SMEM),
        scratch_shapes=[
            pltpu.SMEM((strips,), jnp.int32),
            pltpu.SMEM((strips,), jnp.int32),
            pltpu.SMEM((strips,), jnp.int32),
            pltpu.VMEM((2 * rows, LANES), F32),
            pltpu.VMEM((strips, strip_rows, block_cols), F32),
            pltpu.SMEM((peers,), jnp.int32),
            pltpu.SMEM((CAP * peers,), jnp.int32),
            pltpu.SemaphoreType.DMA((6,)),
        ],
        name="pack",
    )(targets, row_offset, col_block, template, science)

    arrived = lax.all_to_all(payload, "patch", split_axis=0, concat_axis=0, tiled=True)

    frame, col_taps, row_taps, mask = pl.pallas_call(
        prep_kernel,
        out_shape=(
            pltpu.VMEM(((blocks + 1) * height, LANES), F32),
            pltpu.VMEM((bases, 2 * LANES, LANES), BF16),
            pltpu.VMEM((bases * SUBS, 2 * LANES), BF16),
            pltpu.VMEM((blocks * height, LANES), F32),
        ),
        in_specs=[VMEM, VMEM, VMEM, VMEM, VMEM],
        out_specs=(VMEM, VMEM, VMEM, VMEM),
        scratch_shapes=[pltpu.VMEM((32, LANES), F32), pltpu.VMEM((LANES, LANES), F32)],
        name="prep",
    )(template, basis_rows.T, basis_cols.T, stamp_rows, stamp_cols)

    per = VISITS * SUBS
    residual = pl.pallas_call(
        main_kernel,
        in_specs=[VMEM, VMEM, VMEM, VMEM, VMEM],
        out_specs=VMEM,
        scratch_shapes=[
            pltpu.VMEM(((blocks + 1) * height, LANES), F32),
            pltpu.VMEM((per, LANES), F32),
            pltpu.VMEM((bases, per, 2 * LANES), F32),
            pltpu.VMEM((32 * PITCH, LANES), F32),
            pltpu.VMEM((VISITS, 2 * LANES, 2 * LANES), BF16),
            pltpu.VMEM((VISITS, 32, LANES), F32),
        ],
        out_shape=jax.ShapeDtypeStruct((peers, SUBS, LANES), F32),
        compiler_params=pltpu.CompilerParams(vmem_limit_bytes=24 << 20),
        name="fit",
    )(arrived, frame, col_taps, row_taps, mask)

    returned = lax.all_to_all(residual, "patch", split_axis=0, concat_axis=0, tiled=True)

    return pl.pallas_call(
        unpack_kernel,
        out_shape=jax.ShapeDtypeStruct(science.shape, F32),
        in_specs=[SMEM, VMEM],
        out_specs=VMEM,
        compiler_params=pltpu.CompilerParams(vmem_limit_bytes=8 << 20),
        name="unpack",
    )(slots, returned)


def solution(mesh):
    placed = (
        P(None, ("groups", "patch")),
        P(("groups", "patch"), None, None),
        P(("groups", "patch"), None),
        P(("groups", "patch")),
        P(("groups", "patch")),
        P(),
        P(),
        P("groups", None),
        P("groups", None),
    )
    return jax.shard_map(
        on_device,
        mesh=mesh,
        in_specs=placed,
        out_specs=P(("groups", "patch"), None, None),
        check_vma=False,
    )
```

```python
import jax
import jax.numpy as jnp
from jax import lax
from jax.experimental import pallas as pl
from jax.experimental.pallas import tpu as pltpu
from jax.sharding import PartitionSpec as P

CAP = 2
STAMP_HALF = 10
RIDGE = 1.0
LANES = 128
SUBS = 8
VISITS = 16
PITCH = VISITS * SUBS + 8

F32 = jnp.float32
BF16 = jnp.bfloat16
NT = (((1,), (1,)), ((), ()))


def iota(shape, dim):
    return lax.broadcasted_iota(jnp.int32, shape, dim)


def split(x):
    high = x.astype(BF16)
    return high, (x - high.astype(F32)).astype(BF16)


INFO_ROW = 2
SHIFT = 10
TOP = 16
AHEAD = 4
HEIGHT = 40


def pack_kernel(
    dest_hbm, row_hbm, col_hbm, template_hbm, science_hbm, out_ref, slot_ref,
    dest_ref, row_ref, col_ref, edge, science_ref, count, source, sems,
):
    peers = out_ref.shape[0]
    strips = science_ref.shape[0]
    own = lax.axis_index("patch")
    rows = LANES // 2
    last = template_hbm.shape[1] - LANES
    copies = [
        pltpu.make_async_copy(source_ref, target_ref, sems.at[i])
        for i, (source_ref, target_ref) in enumerate(
            (
                (dest_hbm, dest_ref),
                (template_hbm.at[:, 0:LANES], edge.at[0:rows]),
                (template_hbm.at[:, last : last + LANES], edge.at[rows : 2 * rows]),
                (row_hbm, row_ref),
                (col_hbm, col_ref),
                (science_hbm, science_ref),
            )
        )
    ]
    for copy in copies:
        copy.start()

    def clear(d, _):
        count[d] = 0
        for r in range(CAP):
            source[CAP * d + r] = -1
        return 0

    lax.fori_loop(0, peers, clear, 0, unroll=min(peers, 16))

    def place(s, _):
        d = dest_ref[s]
        rank = count[d]
        source[CAP * d + rank] = s
        slot_ref[s] = CAP * d + rank
        count[d] = rank + 1
        return 0

    copies[0].wait()
    lax.fori_loop(0, strips, place, 0, unroll=min(strips, 16))
    for copy in copies[1:]:
        copy.wait()

    edges = edge[...].T
    lane = iota((SUBS, LANES), 1)
    sub = iota((SUBS, LANES), 0)
    low = lane < rows
    head = jnp.where(low, edges[0:8], pltpu.roll(edges[8:16], rows, 1))
    tail = jnp.where(low, pltpu.roll(edges[120:128], rows, 1), edges[112:120])
    info_here = (~low) & (sub == INFO_ROW)

    def fill(d, _):
        halo = jnp.where(d == own + 1, tail, head)
        info = jnp.zeros((SUBS, LANES), F32)
        parts = []
        for r in range(CAP):
            s = source[CAP * d + r]
            live = s >= 0
            at = jnp.maximum(s, 0)
            strip = science_ref[at]
            parts.append(jnp.where(live, strip, 0.0))
            values = (row_ref[at], col_ref[at], jnp.int32(1))
            for j, value in enumerate(values):
                value = jnp.where(live, value, 0).astype(F32)
                info = jnp.where(lane == rows + 3 * r + j, value, info)
        out_ref[d, 0:SUBS, :] = jnp.concatenate(parts, axis=0)
        out_ref[d, SUBS : 2 * SUBS, :] = jnp.where(info_here, info, halo)
        return 0

    lax.fori_loop(0, peers, fill, 0, unroll=min(peers, 16))


def prep_kernel(
    template_ref, rows_ref, cols_ref, stamp_r_ref, stamp_c_ref, frame_ref, col_taps_ref, row_taps_ref, mask_ref, pad_c, pad_t
):
    taps, bases = rows_ref.shape
    own = lax.axis_index("patch")
    rows = template_ref.shape[0]
    height = rows + HEIGHT
    blocks = frame_ref.shape[0] // height
    starts = iota((rows, LANES), 1) < SHIFT
    before = jnp.zeros((rows, LANES), F32)
    for c in range(blocks):
        here = jnp.zeros((rows, LANES), F32)
        if c < blocks - 1:
            here = pltpu.roll(template_ref[:, LANES * c : LANES * (c + 1)], SHIFT, 1)
        at = height * c
        frame_ref[at : at + TOP, :] = jnp.zeros((TOP, LANES), F32)
        frame_ref[at + TOP : at + TOP + rows, :] = jnp.where(starts, before, here)
        frame_ref[at + TOP + rows : at + height, :] = jnp.zeros((HEIGHT - TOP, LANES), F32)
        before = here
    sub_rows = rows
    blocks = blocks - 1
    sub_cols = blocks * LANES
    centre_r = stamp_r_ref[pl.ds(own, 1), :]
    centre_c = stamp_c_ref[pl.ds(own, 1), :]
    stamps = centre_r.shape[1]
    row_hit = (jnp.abs(iota((sub_rows, stamps), 0) - centre_r) <= STAMP_HALF).astype(F32).astype(BF16)
    col_hit = (jnp.abs(iota((sub_cols, stamps), 0) - centre_c) <= STAMP_HALF).astype(F32).astype(BF16)
    counts = lax.dot_general(row_hit, col_hit, NT, preferred_element_type=F32)
    for c in range(blocks):
        at = height * c
        mask_ref[at : at + height, :] = jnp.zeros((height, LANES), F32)
        mask_ref[at + TOP - SHIFT : at + TOP - SHIFT + rows, :] = jnp.minimum(counts[:, LANES * c : LANES * (c + 1)], 1.0)
    pad_t[...] = jnp.zeros_like(pad_t)
    pad_t[0:taps, 0:bases] = cols_ref[...]
    pad_t[32 : 32 + taps, 0:bases] = rows_ref[...]
    filters = pad_t[...].T
    pad_c[...] = jnp.where(iota((32, LANES), 1) < 32, filters[0:32], 0.0)
    full = jnp.where(iota((32, LANES), 1) < 32, pltpu.roll(filters[0:32], LANES - 32, 1), 0.0)
    high = full.astype(BF16).astype(F32)
    base = high + pltpu.roll(high, 32, 1) + pltpu.roll(full - high, 64, 1)
    wide = jnp.concatenate([base, jnp.zeros_like(base)], axis=1)
    lower = iota((SUBS, 2 * LANES), 0) < SUBS // CAP
    tiles = []
    for k in range(bases):
        row = jnp.broadcast_to(wide[k : k + 1, :], (SUBS, 2 * LANES))
        row = pltpu.roll(row, 0, 1, stride=1, stride_axis=0)
        row = jnp.where(lower, row, pltpu.roll(row, 96 - SUBS // CAP, 1))
        tiles.append(row)
    row_taps_ref[...] = jnp.concatenate(tiles, axis=0).astype(BF16)
    def column(k, _):
        ring = jnp.broadcast_to(pad_c[pl.ds(k, 1), :], (LANES, LANES))
        high, low = split(pltpu.roll(ring, 0, 1, stride=1, stride_axis=0))
        col_taps_ref[k, 0:LANES, :] = high
        col_taps_ref[k, LANES : 2 * LANES, :] = low
        return 0

    lax.fori_loop(0, bases, column, 0, unroll=9)


def main_kernel(
    arrived_ref, frame_ref, col_taps_ref, row_taps_ref, mask_ref, out_ref, frame,
    weight, field, design, pairs, gram,
):
    own = lax.axis_index("patch")
    peers = arrived_ref.shape[0]
    bases = col_taps_ref.shape[0]
    rows = LANES // 2
    last = frame.shape[0] - rows - HEIGHT
    per = VISITS * SUBS

    left = jnp.where(own > 0, arrived_ref[jnp.maximum(own - 1, 0), SUBS : 2 * SUBS, :], 0.0)
    right = jnp.where(own < peers - 1, arrived_ref[jnp.minimum(own + 1, peers - 1), SUBS : 2 * SUBS, :], 0.0)
    gap = jnp.zeros((LANES - 4 * SUBS, LANES), F32)
    halo = jnp.concatenate([pltpu.roll(right, 64, 1), right, gap, pltpu.roll(left, 64, 1), left], axis=0).T
    halo = pltpu.roll(halo, SHIFT, 1)
    starts = iota((rows, LANES), 1) < SHIFT
    first_rows = slice(TOP, TOP + rows)
    last_rows = slice(last + TOP, last + TOP + rows)
    frame[first_rows, :] = jnp.where(starts, halo[0:rows], frame_ref[first_rows, :])
    frame[last_rows, :] = jnp.where(starts, frame_ref[last_rows, :], halo[rows : 2 * rows])

    def fit_group(group, _):
        fit_visits(
            group, arrived_ref, col_taps_ref, row_taps_ref, mask_ref, out_ref,
            frame, weight, field, design, pairs, gram,
        )
        return 0

    if peers == VISITS:
        fit_group(0, 0)
    else:
        lax.fori_loop(0, peers // VISITS, fit_group, 0)


def fit_visits(
    group, arrived_ref, col_taps_ref, row_taps_ref, mask_ref, out_ref,
    frame, weight, field, design, pairs, gram,
):
    bases = col_taps_ref.shape[0]
    columns = bases + 1
    per = VISITS * SUBS
    row_taps = row_taps_ref[:, 0:192]

    height = LANES // 2 + HEIGHT
    info = arrived_ref[pl.ds(group * VISITS, VISITS), SUBS + INFO_ROW, :]
    block = pltpu.roll(info, LANES - 1, 1)
    live = pltpu.roll(info, LANES - 2, 1)
    places = jnp.where(live > 0.0, block * height + info + (TOP - SHIFT), height - 32.0).astype(jnp.int32)

    for b in range(VISITS):
        terms = []
        masks = []
        for r in range(CAP):
            first = places[b, LANES // 2 + 3 * r]
            sides = [frame[pl.ds(first + height * side, 32), :] for side in range(2)]
            high, low = split(jnp.concatenate(sides, axis=1))
            terms += [high, low, high]
            masks.append(mask_ref[pl.ds(first, SUBS), :][0 : SUBS // CAP])
        at = slice(SUBS * b, SUBS * (b + 1))
        weight[at, :] = jnp.concatenate(masks, axis=0)
        across = jnp.dot(row_taps, jnp.concatenate(terms, axis=0), preferred_element_type=F32)
        for k in range(bases):
            field[k, at, :] = across[SUBS * k : SUBS * (k + 1)]

    turn = LANES - 32
    inside = iota((32, LANES), 1) >= iota((32, LANES), 0) + turn

    def convolve_cols(k, _):
        bands = []
        for term in range(2):
            ring = col_taps_ref[k, LANES * term : LANES * (term + 1), :]
            ends = ring[turn:]
            none = jnp.zeros_like(ends)
            here = jnp.concatenate([ring[0:turn], jnp.where(inside, ends, none)], axis=0)
            beyond = jnp.concatenate([jnp.zeros_like(ring[0:turn]), jnp.where(inside, none, ends)], axis=0)
            bands.append(jnp.concatenate([here, beyond], axis=1))
        both = jnp.concatenate(split(field[k]), axis=0)
        out = lax.dot_general(both, jnp.concatenate(bands, axis=0), NT, preferred_element_type=F32)
        conv = (out[0:per, LANES:] + out[per:, 0:LANES]) + out[0:per, 0:LANES]
        design[pl.ds(PITCH * k, per), :] = conv
        return 0

    lax.fori_loop(0, bases, convolve_cols, 0, unroll=bases)
    science = arrived_ref[pl.ds(group * VISITS, VISITS), 0:SUBS, :].reshape(per, LANES)
    design[PITCH * bases : PITCH * bases + per, :] = jnp.ones((per, LANES), F32)
    design[PITCH * columns : PITCH * columns + per, :] = science
    design[PITCH * (columns + 1) :, :] = jnp.zeros((design.shape[0] - PITCH * (columns + 1), LANES), F32)

    def gram_of(b, _):
        left, right = [], []
        for q in range(SUBS):
            high, low = split(design[pl.ds(SUBS * b + q, 32, stride=PITCH), :])
            hit = jnp.broadcast_to(weight[pl.ds(SUBS * b + q, 1), :], (2 * SUBS, LANES)).astype(BF16)
            both = jnp.concatenate([high, low], axis=0)
            left.append(jnp.concatenate([both[16 * i : 16 * (i + 1)] * hit for i in range(4)], axis=0))
            right.append(both)
            pairs[b, 32 * q : 32 * (q + 1), 0:LANES] = high
            pairs[b, 32 * q : 32 * (q + 1), LANES:] = low
        left = jnp.concatenate(left, axis=1)
        right = jnp.concatenate(right, axis=1)
        out = lax.dot_general(left, right, NT, preferred_element_type=F32)
        halves = out[32:64] + out[0:32]
        gram[pl.ds(b, 32, stride=VISITS), :] = jnp.concatenate([halves, jnp.zeros((32, LANES - 64), F32)], axis=1)
        return 0

    lax.fori_loop(0, VISITS, gram_of, 0, unroll=VISITS)

    groups = [gram[per * g : per * (g + 1), :].T for g in range(4)]
    groups = [group[0:32] + group[32:64] for group in groups]
    lane = iota((32, LANES), 1)
    sub = iota((32, LANES), 0)
    for g in range(4):
        diagonal = (sub == 8 * g + lane // VISITS) & (sub < columns)
        groups[g] = groups[g] + jnp.where(diagonal, RIDGE, 0.0)
    visit = lane % VISITS

    def spread(p):
        ends = min(SUBS * (p + 1), columns + 1)
        return {j: jnp.take_along_axis(groups[p], visit + VISITS * (j - SUBS * p), axis=1) for j in range(SUBS * p, ends)}

    scale = jnp.zeros((32, LANES), F32)
    panel = spread(0)
    for k in range(columns):
        p = k // SUBS
        if k % SUBS == SUBS - AHEAD and p < 3:
            panel.update(spread(p + 1))
        here = sub == k
        column = panel.pop(k)
        inverse = 1.0 / column[k : k + 1, :]
        scaled = jnp.where(here, 0.0, column * inverse)
        scale = jnp.where(here, inverse, scale)
        for j in panel:
            panel[j] = panel[j] - scaled * panel[j][k : k + 1, :]
        for g in range(p + 1, 4):
            if SUBS * g not in panel:
                groups[g] = groups[g] - scaled * groups[g][k : k + 1, :]
    answer = panel[columns] * scale
    tiled = jnp.concatenate([answer] * 4, axis=0).T

    row = iota((SUBS, LANES), 0)
    side = iota((SUBS, LANES), 1) // 32
    for b in range(VISITS):
        own_rows = jnp.broadcast_to(tiled[b : b + 1], (SUBS, LANES))
        spread = jnp.concatenate([jnp.where(side == row, own_rows, 0.0), jnp.where(side + 4 == row, own_rows, 0.0)], axis=1)
        high = spread.astype(BF16).astype(F32)
        terms = jnp.concatenate([high, spread - high], axis=0).astype(BF16)
        out = lax.dot_general(terms, pairs[b], (((1,), (0,)), ((), ())), preferred_element_type=F32)
        model = (out[0:SUBS, LANES:] + out[SUBS:, 0:LANES]) + out[0:SUBS, 0:LANES]
        out_ref[group * VISITS + b] = science[SUBS * b : SUBS * (b + 1)] - model


def unpack_kernel(slot_ref, back_ref, out_ref):
    strips = out_ref.shape[0]
    half = SUBS // CAP

    def pick(s, _):
        slot = slot_ref[s]
        both = back_ref[slot // CAP]
        out_ref[s] = jnp.where(slot % CAP == 0, both[0:half], both[half:SUBS])
        return 0

    lax.fori_loop(0, strips, pick, 0, unroll=min(strips, 16))


VMEM = pl.BlockSpec(memory_space=pltpu.VMEM)
SMEM = pl.BlockSpec(memory_space=pltpu.SMEM)
ANY = pl.BlockSpec(memory_space=pl.ANY)


def on_device(
    template, science, dest, row_offset, col_block, basis_rows, basis_cols, stamp_rows, stamp_cols
):
    peers = lax.axis_size("patch")
    rows, cols = template.shape
    strips, strip_rows, block_cols = science.shape
    bases = basis_rows.shape[0]
    blocks = cols // LANES
    height = rows + HEIGHT
    targets = dest.reshape(strips)

    kept = pltpu.VMEM if peers <= VISITS else jax.ShapeDtypeStruct
    payload, slots = pl.pallas_call(
        pack_kernel,
        out_shape=(kept((peers, 2 * SUBS, LANES), F32), pltpu.SMEM((strips,), jnp.int32)),
        in_specs=[ANY, ANY, ANY, ANY, ANY],
        out_specs=(VMEM, SMEM),
        scratch_shapes=[
            pltpu.SMEM((strips,), jnp.int32),
            pltpu.SMEM((strips,), jnp.int32),
            pltpu.SMEM((strips,), jnp.int32),
            pltpu.VMEM((2 * rows, LANES), F32),
            pltpu.VMEM((strips, strip_rows, block_cols), F32),
            pltpu.SMEM((peers,), jnp.int32),
            pltpu.SMEM((CAP * peers,), jnp.int32),
            pltpu.SemaphoreType.DMA((6,)),
        ],
        name="pack",
    )(targets, row_offset, col_block, template, science)

    arrived = lax.all_to_all(payload, "patch", split_axis=0, concat_axis=0, tiled=True)

    frame, col_taps, row_taps, mask = pl.pallas_call(
        prep_kernel,
        out_shape=(
            pltpu.VMEM(((blocks + 1) * height, LANES), F32),
            pltpu.VMEM((bases, 2 * LANES, LANES), BF16),
            pltpu.VMEM((bases * SUBS, 2 * LANES), BF16),
            pltpu.VMEM((blocks * height, LANES), F32),
        ),
        in_specs=[VMEM, VMEM, VMEM, VMEM, VMEM],
        out_specs=(VMEM, VMEM, VMEM, VMEM),
        scratch_shapes=[pltpu.VMEM((32, LANES), F32), pltpu.VMEM((LANES, LANES), F32)],
        name="prep",
    )(template, basis_rows.T, basis_cols.T, stamp_rows, stamp_cols)

    per = VISITS * SUBS
    residual, _ = pl.pallas_call(
        main_kernel,
        in_specs=[VMEM, VMEM, VMEM, VMEM, VMEM],
        out_specs=(VMEM, VMEM),
        scratch_shapes=[
            pltpu.VMEM((per, LANES), F32),
            pltpu.VMEM((bases, per, 2 * LANES), F32),
            pltpu.VMEM((32 * PITCH, LANES), F32),
            pltpu.VMEM((VISITS, 2 * LANES, 2 * LANES), BF16),
            pltpu.VMEM((VISITS * 32, LANES), F32),
        ],
        out_shape=(jax.ShapeDtypeStruct((peers, SUBS, LANES), F32), pltpu.VMEM(((blocks + 1) * height, LANES), F32)),
        input_output_aliases={1: 1},
        compiler_params=pltpu.CompilerParams(vmem_limit_bytes=24 << 20),
        name="fit",
    )(arrived, frame, col_taps, row_taps, mask)

    returned = lax.all_to_all(residual, "patch", split_axis=0, concat_axis=0, tiled=True)

    return pl.pallas_call(
        unpack_kernel,
        out_shape=jax.ShapeDtypeStruct(science.shape, F32),
        in_specs=[SMEM, VMEM],
        out_specs=VMEM,
        compiler_params=pltpu.CompilerParams(vmem_limit_bytes=8 << 20),
        name="unpack",
    )(slots, returned)


def solution(mesh):
    placed = (
        P(None, ("groups", "patch")),
        P(("groups", "patch"), None, None),
        P(("groups", "patch"), None),
        P(("groups", "patch")),
        P(("groups", "patch")),
        P(),
        P(),
        P("groups", None),
        P("groups", None),
    )
    return jax.shard_map(
        on_device,
        mesh=mesh,
        in_specs=placed,
        out_specs=P(("groups", "patch"), None, None),
        check_vma=False,
    )
```

```python
import jax
import jax.numpy as jnp
from jax import lax
from jax.experimental import pallas as pl
from jax.experimental.pallas import tpu as pltpu
from jax.sharding import PartitionSpec as P

CAP = 2
STAMP_HALF = 10
RIDGE = 1.0
LANES = 128
SUBS = 8
VISITS = 16
PITCH = VISITS * SUBS + 8

F32 = jnp.float32
BF16 = jnp.bfloat16
NT = (((1,), (1,)), ((), ()))


def iota(shape, dim):
    return lax.broadcasted_iota(jnp.int32, shape, dim)


def split(x):
    high = x.astype(BF16)
    return high, (x - high.astype(F32)).astype(BF16)


PARCEL = 14
SHIFT = 10
TOP = 16
AHEAD = 4
HEIGHT = 40


def pack_kernel(
    dest_hbm, row_hbm, col_hbm, template_hbm, science_hbm, out_ref, slot_ref,
    dest_ref, row_ref, col_ref, edge, science_ref, count, source, sems,
):
    peers = out_ref.shape[0] // PARCEL
    strips = science_ref.shape[0]
    own = lax.axis_index("patch")
    rows = LANES // 2
    last = template_hbm.shape[1] - LANES
    copies = [
        pltpu.make_async_copy(source_ref, target_ref, sems.at[i])
        for i, (source_ref, target_ref) in enumerate(
            (
                (dest_hbm, dest_ref),
                (template_hbm.at[:, 0:LANES], edge.at[0:rows]),
                (template_hbm.at[:, last : last + LANES], edge.at[rows : 2 * rows]),
                (row_hbm, row_ref),
                (col_hbm, col_ref),
                (science_hbm, science_ref),
            )
        )
    ]
    for copy in copies:
        copy.start()

    def clear(d, _):
        count[d] = 0
        for r in range(CAP):
            source[CAP * d + r] = -1
        return 0

    lax.fori_loop(0, peers, clear, 0, unroll=min(peers, 16))

    def place(s, _):
        d = dest_ref[s]
        rank = count[d]
        source[CAP * d + rank] = s
        slot_ref[s] = CAP * d + rank
        count[d] = rank + 1
        return 0

    copies[0].wait()
    lax.fori_loop(0, strips, place, 0, unroll=min(strips, 16))
    for copy in copies[1:]:
        copy.wait()

    edges = edge[...].T
    lane = iota((SUBS, LANES), 1)
    sub = iota((SUBS, LANES), 0)
    low = lane < rows
    head = jnp.where(low, edges[0:8], pltpu.roll(edges[5:13], rows, 1))
    tail = jnp.where(low, pltpu.roll(edges[118:126], rows, 1), jnp.concatenate([edges[123:128], edges[0:3]], axis=0))
    info_here = sub == PARCEL - 1 - SUBS

    def fill(d, _):
        halo = jnp.where(d == own + 1, tail, head)
        info = jnp.zeros((SUBS, LANES), F32)
        parts = []
        for r in range(CAP):
            s = source[CAP * d + r]
            live = s >= 0
            at = jnp.maximum(s, 0)
            strip = science_ref[at]
            parts.append(jnp.where(live, strip, 0.0))
            values = (row_ref[at], col_ref[at], jnp.int32(1))
            for j, value in enumerate(values):
                value = jnp.where(live, value, 0).astype(F32)
                info = jnp.where(lane == 3 * r + j, value, info)
        out_ref[pl.ds(PARCEL * d, SUBS), :] = jnp.concatenate(parts, axis=0)
        out_ref[pl.ds(PARCEL * d + SUBS, PARCEL - SUBS), :] = jnp.where(info_here, info, halo)[0 : PARCEL - SUBS]
        return 0

    lax.fori_loop(0, peers, fill, 0, unroll=min(peers, 16))


def prep_kernel(
    template_ref, rows_ref, cols_ref, stamp_r_ref, stamp_c_ref, frame_ref, col_taps_ref, row_taps_ref, mask_ref, pad_c, pad_t
):
    taps, bases = rows_ref.shape
    own = lax.axis_index("patch")
    rows = template_ref.shape[0]
    height = rows + HEIGHT
    blocks = frame_ref.shape[0] // height
    starts = iota((rows, LANES), 1) < SHIFT
    before = jnp.zeros((rows, LANES), F32)
    for c in range(blocks):
        here = jnp.zeros((rows, LANES), F32)
        if c < blocks - 1:
            here = pltpu.roll(template_ref[:, LANES * c : LANES * (c + 1)], SHIFT, 1)
        at = height * c
        frame_ref[at : at + TOP, :] = jnp.zeros((TOP, LANES), F32)
        frame_ref[at + TOP : at + TOP + rows, :] = jnp.where(starts, before, here)
        frame_ref[at + TOP + rows : at + height, :] = jnp.zeros((HEIGHT - TOP, LANES), F32)
        before = here
    sub_rows = rows
    blocks = blocks - 1
    sub_cols = blocks * LANES
    centre_r = stamp_r_ref[pl.ds(own, 1), :]
    centre_c = stamp_c_ref[pl.ds(own, 1), :]
    stamps = centre_r.shape[1]
    row_hit = (jnp.abs(iota((sub_rows, stamps), 0) - centre_r) <= STAMP_HALF).astype(F32).astype(BF16)
    col_hit = (jnp.abs(iota((sub_cols, stamps), 0) - centre_c) <= STAMP_HALF).astype(F32).astype(BF16)
    counts = lax.dot_general(row_hit, col_hit, NT, preferred_element_type=F32)
    for c in range(blocks):
        at = height * c
        mask_ref[at : at + height, :] = jnp.zeros((height, LANES), F32)
        mask_ref[at + TOP - SHIFT : at + TOP - SHIFT + rows, :] = jnp.minimum(counts[:, LANES * c : LANES * (c + 1)], 1.0)
    pad_t[...] = jnp.zeros_like(pad_t)
    pad_t[0:taps, 0:bases] = cols_ref[...]
    pad_t[32 : 32 + taps, 0:bases] = rows_ref[...]
    filters = pad_t[...].T
    pad_c[...] = jnp.where(iota((32, LANES), 1) < 32, filters[0:32], 0.0)
    full = jnp.where(iota((32, LANES), 1) < 32, pltpu.roll(filters[0:32], LANES - 32, 1), 0.0)
    high = full.astype(BF16).astype(F32)
    base = high + pltpu.roll(high, 32, 1) + pltpu.roll(full - high, 64, 1)
    wide = jnp.concatenate([base, jnp.zeros_like(base)], axis=1)
    lower = iota((SUBS, 2 * LANES), 0) < SUBS // CAP
    tiles = []
    for k in range(bases):
        row = jnp.broadcast_to(wide[k : k + 1, :], (SUBS, 2 * LANES))
        row = pltpu.roll(row, 0, 1, stride=1, stride_axis=0)
        row = jnp.where(lower, row, pltpu.roll(row, 96 - SUBS // CAP, 1))
        tiles.append(row)
    row_taps_ref[...] = jnp.concatenate(tiles, axis=0).astype(BF16)
    def column(k, _):
        ring = jnp.broadcast_to(pad_c[pl.ds(k, 1), :], (LANES, LANES))
        high, low = split(pltpu.roll(ring, 0, 1, stride=1, stride_axis=0))
        col_taps_ref[k, 0:LANES, :] = high
        col_taps_ref[k, LANES : 2 * LANES, :] = low
        return 0

    lax.fori_loop(0, bases, column, 0, unroll=9)


def main_kernel(
    arrived_ref, frame_ref, col_taps_ref, row_taps_ref, mask_ref, out_ref, frame,
    weight, field, design, pairs, gram,
):
    own = lax.axis_index("patch")
    peers = out_ref.shape[0]
    bases = col_taps_ref.shape[0]
    rows = LANES // 2
    last = frame.shape[0] - rows - HEIGHT
    per = VISITS * SUBS

    skip = PARCEL - SUBS
    left = arrived_ref[pl.ds(PARCEL * jnp.maximum(own - 1, 0) + skip, SUBS), :]
    right = arrived_ref[pl.ds(PARCEL * jnp.minimum(own + 1, peers - 1) + skip, SUBS), :]
    left = jnp.where(own > 0, left, 0.0)
    right = jnp.where(own < peers - 1, right, 0.0)
    pick = slice(SUBS - skip, SUBS - 1)
    ends = [tile[pick] for tile in (pltpu.roll(right, rows, 1), right, left, pltpu.roll(left, rows, 1))]
    gap = jnp.zeros((LANES - 2 * SHIFT, LANES), F32)
    halo = jnp.concatenate([ends[0], ends[1], gap, ends[2], ends[3]], axis=0).T
    halo = pltpu.roll(halo, SHIFT, 1)
    starts = iota((rows, LANES), 1) < SHIFT
    first_rows = slice(TOP, TOP + rows)
    last_rows = slice(last + TOP, last + TOP + rows)
    frame[first_rows, :] = jnp.where(starts, halo[0:rows], frame_ref[first_rows, :])
    frame[last_rows, :] = jnp.where(starts, frame_ref[last_rows, :], halo[rows : 2 * rows])

    def fit_group(group, _):
        fit_visits(
            group, arrived_ref, col_taps_ref, row_taps_ref, mask_ref, out_ref,
            frame, weight, field, design, pairs, gram,
        )
        return 0

    if peers == VISITS:
        fit_group(0, 0)
    else:
        lax.fori_loop(0, peers // VISITS, fit_group, 0)


def fit_visits(
    group, arrived_ref, col_taps_ref, row_taps_ref, mask_ref, out_ref,
    frame, weight, field, design, pairs, gram,
):
    bases = col_taps_ref.shape[0]
    columns = bases + 1
    per = VISITS * SUBS
    row_taps = row_taps_ref[:, 0:192]

    height = LANES // 2 + HEIGHT
    start = group * (VISITS * PARCEL)
    info = arrived_ref[pl.ds(start + PARCEL - 1, VISITS, stride=PARCEL), :]
    block = pltpu.roll(info, LANES - 1, 1)
    live = pltpu.roll(info, LANES - 2, 1)
    places = jnp.where(live > 0.0, block * height + info + (TOP - SHIFT), height - 32.0).astype(jnp.int32)

    for b in range(VISITS):
        terms = []
        masks = []
        for r in range(CAP):
            first = places[b, 3 * r]
            sides = [frame[pl.ds(first + height * side, 32), :] for side in range(2)]
            high, low = split(jnp.concatenate(sides, axis=1))
            terms += [high, low, high]
            masks.append(mask_ref[pl.ds(first, SUBS), :][0 : SUBS // CAP])
        at = slice(SUBS * b, SUBS * (b + 1))
        weight[at, :] = jnp.concatenate(masks, axis=0)
        across = jnp.dot(row_taps, jnp.concatenate(terms, axis=0), preferred_element_type=F32)
        for k in range(bases):
            field[k, at, :] = across[SUBS * k : SUBS * (k + 1)]

    turn = LANES - 32
    inside = iota((32, LANES), 1) >= iota((32, LANES), 0) + turn

    def convolve_cols(k, _):
        bands = []
        for term in range(2):
            ring = col_taps_ref[k, LANES * term : LANES * (term + 1), :]
            ends = ring[turn:]
            none = jnp.zeros_like(ends)
            here = jnp.concatenate([ring[0:turn], jnp.where(inside, ends, none)], axis=0)
            beyond = jnp.concatenate([jnp.zeros_like(ring[0:turn]), jnp.where(inside, none, ends)], axis=0)
            bands.append(jnp.concatenate([here, beyond], axis=1))
        both = jnp.concatenate(split(field[k]), axis=0)
        out = lax.dot_general(both, jnp.concatenate(bands, axis=0), NT, preferred_element_type=F32)
        conv = (out[0:per, LANES:] + out[per:, 0:LANES]) + out[0:per, 0:LANES]
        design[pl.ds(PITCH * k, per), :] = conv
        return 0

    lax.fori_loop(0, bases, convolve_cols, 0, unroll=bases)
    science = jnp.concatenate([arrived_ref[pl.ds(start + PARCEL * b, SUBS), :] for b in range(VISITS)], axis=0)
    design[PITCH * bases : PITCH * bases + per, :] = jnp.ones((per, LANES), F32)
    design[PITCH * columns : PITCH * columns + per, :] = science
    design[PITCH * (columns + 1) :, :] = jnp.zeros((design.shape[0] - PITCH * (columns + 1), LANES), F32)

    def gram_of(b, _):
        left, right = [], []
        for q in range(SUBS):
            high, low = split(design[pl.ds(SUBS * b + q, 32, stride=PITCH), :])
            hit = jnp.broadcast_to(weight[pl.ds(SUBS * b + q, 1), :], (2 * SUBS, LANES)).astype(BF16)
            both = jnp.concatenate([high, low], axis=0)
            left.append(jnp.concatenate([both[16 * i : 16 * (i + 1)] * hit for i in range(4)], axis=0))
            right.append(both)
            pairs[b, 32 * q : 32 * (q + 1), 0:LANES] = high
            pairs[b, 32 * q : 32 * (q + 1), LANES:] = low
        left = jnp.concatenate(left, axis=1)
        right = jnp.concatenate(right, axis=1)
        out = lax.dot_general(left, right, NT, preferred_element_type=F32)
        halves = out[32:64] + out[0:32]
        gram[pl.ds(b, 32, stride=VISITS), :] = jnp.concatenate([halves, jnp.zeros((32, LANES - 64), F32)], axis=1)
        return 0

    lax.fori_loop(0, VISITS, gram_of, 0, unroll=VISITS)

    groups = [gram[per * g : per * (g + 1), :].T for g in range(4)]
    groups = [group[0:32] + group[32:64] for group in groups]
    lane = iota((32, LANES), 1)
    sub = iota((32, LANES), 0)
    for g in range(4):
        diagonal = (sub == 8 * g + lane // VISITS) & (sub < columns)
        groups[g] = groups[g] + jnp.where(diagonal, RIDGE, 0.0)
    visit = lane % VISITS

    def spread(p):
        ends = min(SUBS * (p + 1), columns + 1)
        return {j: jnp.take_along_axis(groups[p], visit + VISITS * (j - SUBS * p), axis=1) for j in range(SUBS * p, ends)}

    scale = jnp.zeros((32, LANES), F32)
    panel = spread(0)
    for k in range(columns):
        p = k // SUBS
        if k % SUBS == SUBS - AHEAD and p < 3:
            panel.update(spread(p + 1))
        here = sub == k
        column = panel.pop(k)
        inverse = 1.0 / column[k : k + 1, :]
        scaled = jnp.where(here, 0.0, column * inverse)
        scale = jnp.where(here, inverse, scale)
        for j in panel:
            panel[j] = panel[j] - scaled * panel[j][k : k + 1, :]
        for g in range(p + 1, 4):
            if SUBS * g not in panel:
                groups[g] = groups[g] - scaled * groups[g][k : k + 1, :]
    answer = panel[columns] * scale
    tiled = jnp.concatenate([answer] * 4, axis=0).T

    row = iota((SUBS, LANES), 0)
    side = iota((SUBS, LANES), 1) // 32
    for b in range(VISITS):
        own_rows = jnp.broadcast_to(tiled[b : b + 1], (SUBS, LANES))
        spread = jnp.concatenate([jnp.where(side == row, own_rows, 0.0), jnp.where(side + 4 == row, own_rows, 0.0)], axis=1)
        high = spread.astype(BF16).astype(F32)
        terms = jnp.concatenate([high, spread - high], axis=0).astype(BF16)
        out = lax.dot_general(terms, pairs[b], (((1,), (0,)), ((), ())), preferred_element_type=F32)
        model = (out[0:SUBS, LANES:] + out[SUBS:, 0:LANES]) + out[0:SUBS, 0:LANES]
        out_ref[group * VISITS + b] = science[SUBS * b : SUBS * (b + 1)] - model


def unpack_kernel(slot_ref, back_ref, out_ref):
    strips = out_ref.shape[0]
    half = SUBS // CAP

    def pick(s, _):
        slot = slot_ref[s]
        both = back_ref[slot // CAP]
        out_ref[s] = jnp.where(slot % CAP == 0, both[0:half], both[half:SUBS])
        return 0

    lax.fori_loop(0, strips, pick, 0, unroll=min(strips, 16))


VMEM = pl.BlockSpec(memory_space=pltpu.VMEM)
SMEM = pl.BlockSpec(memory_space=pltpu.SMEM)
ANY = pl.BlockSpec(memory_space=pl.ANY)


def on_device(
    template, science, dest, row_offset, col_block, basis_rows, basis_cols, stamp_rows, stamp_cols
):
    peers = lax.axis_size("patch")
    rows, cols = template.shape
    strips, strip_rows, block_cols = science.shape
    bases = basis_rows.shape[0]
    blocks = cols // LANES
    height = rows + HEIGHT
    targets = dest.reshape(strips)

    kept = pltpu.VMEM if peers <= VISITS else jax.ShapeDtypeStruct
    payload, slots = pl.pallas_call(
        pack_kernel,
        out_shape=(kept((peers * PARCEL, LANES), F32), pltpu.SMEM((strips,), jnp.int32)),
        in_specs=[ANY, ANY, ANY, ANY, ANY],
        out_specs=(VMEM, SMEM),
        scratch_shapes=[
            pltpu.SMEM((strips,), jnp.int32),
            pltpu.SMEM((strips,), jnp.int32),
            pltpu.SMEM((strips,), jnp.int32),
            pltpu.VMEM((2 * rows, LANES), F32),
            pltpu.VMEM((strips, strip_rows, block_cols), F32),
            pltpu.SMEM((peers,), jnp.int32),
            pltpu.SMEM((CAP * peers,), jnp.int32),
            pltpu.SemaphoreType.DMA((6,)),
        ],
        name="pack",
    )(targets, row_offset, col_block, template, science)

    parcels = payload.reshape(peers, 1, PARCEL * LANES)
    arrived = lax.all_to_all(parcels, "patch", split_axis=0, concat_axis=0, tiled=True).reshape(payload.shape)

    frame, col_taps, row_taps, mask = pl.pallas_call(
        prep_kernel,
        out_shape=(
            pltpu.VMEM(((blocks + 1) * height, LANES), F32),
            pltpu.VMEM((bases, 2 * LANES, LANES), BF16),
            pltpu.VMEM((bases * SUBS, 2 * LANES), BF16),
            pltpu.VMEM((blocks * height, LANES), F32),
        ),
        in_specs=[VMEM, VMEM, VMEM, VMEM, VMEM],
        out_specs=(VMEM, VMEM, VMEM, VMEM),
        scratch_shapes=[pltpu.VMEM((32, LANES), F32), pltpu.VMEM((LANES, LANES), F32)],
        name="prep",
    )(template, basis_rows.T, basis_cols.T, stamp_rows, stamp_cols)

    per = VISITS * SUBS
    residual, _ = pl.pallas_call(
        main_kernel,
        in_specs=[VMEM, VMEM, VMEM, VMEM, VMEM],
        out_specs=(VMEM, VMEM),
        scratch_shapes=[
            pltpu.VMEM((per, LANES), F32),
            pltpu.VMEM((bases, per, 2 * LANES), F32),
            pltpu.VMEM((32 * PITCH, LANES), F32),
            pltpu.VMEM((VISITS, 2 * LANES, 2 * LANES), BF16),
            pltpu.VMEM((VISITS * 32, LANES), F32),
        ],
        out_shape=(jax.ShapeDtypeStruct((peers, SUBS, LANES), F32), pltpu.VMEM(((blocks + 1) * height, LANES), F32)),
        input_output_aliases={1: 1},
        compiler_params=pltpu.CompilerParams(vmem_limit_bytes=24 << 20),
        name="fit",
    )(arrived, frame, col_taps, row_taps, mask)

    returned = lax.all_to_all(residual, "patch", split_axis=0, concat_axis=0, tiled=True)

    return pl.pallas_call(
        unpack_kernel,
        out_shape=jax.ShapeDtypeStruct(science.shape, F32),
        in_specs=[SMEM, VMEM],
        out_specs=VMEM,
        compiler_params=pltpu.CompilerParams(vmem_limit_bytes=8 << 20),
        name="unpack",
    )(slots, returned)


def solution(mesh):
    placed = (
        P(None, ("groups", "patch")),
        P(("groups", "patch"), None, None),
        P(("groups", "patch"), None),
        P(("groups", "patch")),
        P(("groups", "patch")),
        P(),
        P(),
        P("groups", None),
        P("groups", None),
    )
    return jax.shard_map(
        on_device,
        mesh=mesh,
        in_specs=placed,
        out_specs=P(("groups", "patch"), None, None),
        check_vma=False,
    )
```

```python
import jax
import jax.numpy as jnp
from jax import lax
from jax.experimental import pallas as pl
from jax.experimental.pallas import tpu as pltpu
from jax.sharding import PartitionSpec as P

CAP = 2
STAMP_HALF = 10
RIDGE = 1.0
LANES = 128
SUBS = 8
VISITS = 16
PITCH = VISITS * SUBS + 1

F32 = jnp.float32
BF16 = jnp.bfloat16
NT = (((1,), (1,)), ((), ()))


def iota(shape, dim):
    return lax.broadcasted_iota(jnp.int32, shape, dim)


def split(x):
    high = x.astype(BF16)
    return high, (x - high.astype(F32)).astype(BF16)


PARCEL = 14
SHIFT = 10
TOP = 16
AHEAD = 4
HEIGHT = 40


def pack_kernel(
    dest_hbm, row_hbm, col_hbm, template_hbm, science_hbm, out_ref, slot_ref,
    dest_ref, row_ref, col_ref, edge, science_ref, count, source, sems,
):
    peers = out_ref.shape[0] // PARCEL
    strips = science_ref.shape[0]
    own = lax.axis_index("patch")
    rows = LANES // 2
    last = template_hbm.shape[1] - LANES
    copies = [
        pltpu.make_async_copy(source_ref, target_ref, sems.at[i])
        for i, (source_ref, target_ref) in enumerate(
            (
                (dest_hbm, dest_ref),
                (template_hbm.at[:, 0:LANES], edge.at[0:rows]),
                (template_hbm.at[:, last : last + LANES], edge.at[rows : 2 * rows]),
                (row_hbm, row_ref),
                (col_hbm, col_ref),
                (science_hbm, science_ref),
            )
        )
    ]
    for copy in copies:
        copy.start()

    def clear(d, _):
        count[d] = 0
        for r in range(CAP):
            source[CAP * d + r] = -1
        return 0

    lax.fori_loop(0, peers, clear, 0, unroll=min(peers, 16))

    def place(s, _):
        d = dest_ref[s]
        rank = count[d]
        source[CAP * d + rank] = s
        slot_ref[s] = CAP * d + rank
        count[d] = rank + 1
        return 0

    copies[0].wait()
    lax.fori_loop(0, strips, place, 0, unroll=min(strips, 16))
    for copy in copies[1:]:
        copy.wait()

    edges = edge[...].T
    lane = iota((SUBS, LANES), 1)
    sub = iota((SUBS, LANES), 0)
    low = lane < rows
    head = jnp.where(low, edges[0:8], pltpu.roll(edges[5:13], rows, 1))
    tail = jnp.where(low, pltpu.roll(edges[118:126], rows, 1), jnp.concatenate([edges[123:128], edges[0:3]], axis=0))
    info_here = sub == PARCEL - 1 - SUBS

    def fill(d, _):
        halo = jnp.where(d == own + 1, tail, head)
        info = jnp.zeros((SUBS, LANES), F32)
        parts = []
        for r in range(CAP):
            s = source[CAP * d + r]
            live = s >= 0
            at = jnp.maximum(s, 0)
            strip = science_ref[at]
            parts.append(jnp.where(live, strip, 0.0))
            values = (row_ref[at], col_ref[at], jnp.int32(1))
            for j, value in enumerate(values):
                value = jnp.where(live, value, 0).astype(F32)
                info = jnp.where(lane == 3 * r + j, value, info)
        out_ref[pl.ds(PARCEL * d, SUBS), :] = jnp.concatenate(parts, axis=0)
        out_ref[pl.ds(PARCEL * d + SUBS, PARCEL - SUBS), :] = jnp.where(info_here, info, halo)[0 : PARCEL - SUBS]
        return 0

    lax.fori_loop(0, peers, fill, 0, unroll=min(peers, 16))


def prep_kernel(
    template_ref, rows_ref, cols_ref, stamp_r_ref, stamp_c_ref, frame_ref, col_taps_ref, beyond_ref, row_taps_ref, mask_ref, pad_c, pad_t
):
    taps, bases = rows_ref.shape
    own = lax.axis_index("patch")
    rows = template_ref.shape[0]
    height = rows + HEIGHT
    blocks = frame_ref.shape[0] // height
    starts = iota((rows, LANES), 1) < SHIFT
    before = jnp.zeros((rows, LANES), F32)
    for c in range(blocks):
        here = jnp.zeros((rows, LANES), F32)
        if c < blocks - 1:
            here = pltpu.roll(template_ref[:, LANES * c : LANES * (c + 1)], SHIFT, 1)
        at = height * c
        frame_ref[at : at + TOP, :] = jnp.zeros((TOP, LANES), F32)
        frame_ref[at + TOP : at + TOP + rows, :] = jnp.where(starts, before, here)
        frame_ref[at + TOP + rows : at + height, :] = jnp.zeros((HEIGHT - TOP, LANES), F32)
        before = here
    sub_rows = rows
    blocks = blocks - 1
    sub_cols = blocks * LANES
    centre_r = stamp_r_ref[pl.ds(own, 1), :]
    centre_c = stamp_c_ref[pl.ds(own, 1), :]
    stamps = centre_r.shape[1]
    row_hit = (jnp.abs(iota((sub_rows, stamps), 0) - centre_r) <= STAMP_HALF).astype(F32).astype(BF16)
    col_hit = (jnp.abs(iota((sub_cols, stamps), 0) - centre_c) <= STAMP_HALF).astype(F32).astype(BF16)
    counts = lax.dot_general(row_hit, col_hit, NT, preferred_element_type=F32)
    for c in range(blocks):
        at = height * c
        mask_ref[at : at + height, :] = jnp.zeros((height, LANES), F32)
        mask_ref[at + TOP - SHIFT : at + TOP - SHIFT + rows, :] = jnp.minimum(counts[:, LANES * c : LANES * (c + 1)], 1.0)
    pad_t[...] = jnp.zeros_like(pad_t)
    pad_t[0:taps, 0:bases] = cols_ref[...]
    pad_t[32 : 32 + taps, 0:bases] = rows_ref[...]
    filters = pad_t[...].T
    pad_c[...] = jnp.where(iota((32, LANES), 1) < 32, filters[0:32], 0.0)
    full = jnp.where(iota((32, LANES), 1) < 32, pltpu.roll(filters[0:32], LANES - 32, 1), 0.0)
    high = full.astype(BF16).astype(F32)
    base = high + pltpu.roll(high, 32, 1) + pltpu.roll(full - high, 64, 1)
    wide = jnp.concatenate([base, jnp.zeros_like(base)], axis=1)
    lower = iota((SUBS, 2 * LANES), 0) < SUBS // CAP
    tiles = []
    for k in range(bases):
        row = jnp.broadcast_to(wide[k : k + 1, :], (SUBS, 2 * LANES))
        row = pltpu.roll(row, 0, 1, stride=1, stride_axis=0)
        row = jnp.where(lower, row, pltpu.roll(row, 96 - SUBS // CAP, 1))
        tiles.append(row)
    row_taps_ref[...] = jnp.concatenate(tiles, axis=0).astype(BF16)
    within = iota((LANES, LANES), 1) >= iota((LANES, LANES), 0)

    def column(k, _):
        ring = jnp.broadcast_to(pad_c[pl.ds(k, 1), :], (LANES, LANES))
        ring = pltpu.roll(ring, 0, 1, stride=1, stride_axis=0)
        high, low = split(jnp.where(within, ring, 0.0))
        col_taps_ref[k, 0:LANES, :] = high
        col_taps_ref[k, LANES : 2 * LANES, :] = low
        beyond = jnp.where(within, 0.0, ring)[LANES - 32 :]
        beyond = beyond + pltpu.roll(beyond, 32, 1)
        beyond = beyond + pltpu.roll(beyond, 64, 1)
        high, low = split(beyond)
        beyond_ref[k, 0:32, :] = high
        beyond_ref[k, 32:64, :] = low
        return 0

    lax.fori_loop(0, bases, column, 0, unroll=9)


def main_kernel(
    arrived_ref, frame_ref, col_taps_ref, beyond_ref, row_taps_ref, mask_ref, out_ref, frame,
    weight, field, design, pairs, gram,
):
    own = lax.axis_index("patch")
    peers = out_ref.shape[0]
    bases = col_taps_ref.shape[0]
    rows = LANES // 2
    last = frame.shape[0] - rows - HEIGHT
    per = VISITS * SUBS

    skip = PARCEL - SUBS
    left = arrived_ref[pl.ds(PARCEL * jnp.maximum(own - 1, 0) + skip, SUBS), :]
    right = arrived_ref[pl.ds(PARCEL * jnp.minimum(own + 1, peers - 1) + skip, SUBS), :]
    left = jnp.where(own > 0, left, 0.0)
    right = jnp.where(own < peers - 1, right, 0.0)
    pick = slice(SUBS - skip, SUBS - 1)
    ends = [tile[pick] for tile in (pltpu.roll(right, rows, 1), right, left, pltpu.roll(left, rows, 1))]
    gap = jnp.zeros((LANES - 2 * SHIFT, LANES), F32)
    halo = jnp.concatenate([ends[0], ends[1], gap, ends[2], ends[3]], axis=0).T
    halo = pltpu.roll(halo, SHIFT, 1)
    starts = iota((rows, LANES), 1) < SHIFT
    first_rows = slice(TOP, TOP + rows)
    last_rows = slice(last + TOP, last + TOP + rows)
    frame[first_rows, :] = jnp.where(starts, halo[0:rows], frame_ref[first_rows, :])
    frame[last_rows, :] = jnp.where(starts, frame_ref[last_rows, :], halo[rows : 2 * rows])

    def fit_group(group, _):
        fit_visits(
            group, arrived_ref, col_taps_ref, beyond_ref, row_taps_ref, mask_ref, out_ref,
            frame, weight, field, design, pairs, gram,
        )
        return 0

    if peers == VISITS:
        fit_group(0, 0)
    else:
        lax.fori_loop(0, peers // VISITS, fit_group, 0)


def fit_visits(
    group, arrived_ref, col_taps_ref, beyond_ref, row_taps_ref, mask_ref, out_ref,
    frame, weight, field, design, pairs, gram,
):
    bases = col_taps_ref.shape[0]
    columns = bases + 1
    per = VISITS * SUBS
    row_taps = row_taps_ref[:, 0:192]

    height = LANES // 2 + HEIGHT
    start = group * (VISITS * PARCEL)
    info = arrived_ref[pl.ds(start + PARCEL - 1, VISITS, stride=PARCEL), :]
    block = pltpu.roll(info, LANES - 1, 1)
    live = pltpu.roll(info, LANES - 2, 1)
    places = jnp.where(live > 0.0, block * height + info + (TOP - SHIFT), height - 32.0).astype(jnp.int32)

    first = [[places[b, 3 * r] for r in range(CAP)] for b in range(VISITS)]

    def tall(windows):
        terms = []
        for window in windows:
            high, low = split(window)
            terms += [high, low, high]
        return jnp.concatenate(terms, axis=0)

    for b in range(0, VISITS, 2):
        pair = []
        for v in (b, b + 1):
            masks = [mask_ref[pl.ds(at, SUBS), :][0 : SUBS // CAP] for at in first[v]]
            weight[SUBS * v : SUBS * (v + 1), :] = jnp.concatenate(masks, axis=0)
            pair.append(tall([frame[pl.ds(at, 32), :] for at in first[v]]))
        across = jnp.dot(row_taps, jnp.concatenate(pair, axis=1), preferred_element_type=F32)
        for k in range(bases):
            rows = across[SUBS * k : SUBS * (k + 1)]
            field[k, SUBS * b : SUBS * (b + 1), 0:LANES] = rows[:, 0:LANES]
            field[k, SUBS * (b + 1) : SUBS * (b + 2), 0:LANES] = rows[:, LANES:]

    place_of = iota((32, LANES), 1) // 32
    for b in range(0, VISITS, 8):
        sides = []
        for h in range(b, b + 8, 4):
            windows = []
            for r in range(CAP):
                window = frame[pl.ds(first[h][r] + height, 32), :]
                for v in range(1, 4):
                    moved = pltpu.roll(frame[pl.ds(first[h + v][r] + height, 32), :], 32 * v, 1)
                    window = jnp.where(place_of == v, moved, window)
                windows.append(window)
            sides.append(tall(windows))
        across = jnp.dot(row_taps, jnp.concatenate(sides, axis=1), preferred_element_type=F32)
        for k in range(bases):
            for v in range(8):
                rows = across[SUBS * k : SUBS * (k + 1), LANES * (v // 4) : LANES * (v // 4 + 1)]
                rows = jnp.where(place_of[0:SUBS] == v % 4, rows, 0.0)
                field[k, SUBS * (b + v) : SUBS * (b + v + 1), LANES:] = rows

    top = jnp.zeros((LANES - 32, LANES), BF16)

    def convolve_cols(k, _):
        beyond = jnp.concatenate([top, beyond_ref[k, 0:32, :], top, beyond_ref[k, 32:64, :]], axis=0)
        bands = [jnp.concatenate([col_taps_ref[k], beyond], axis=1)]
        both = jnp.concatenate(split(field[k]), axis=0)
        out = lax.dot_general(both, jnp.concatenate(bands, axis=0), NT, preferred_element_type=F32)
        conv = (out[0:per, LANES:] + out[per:, 0:LANES]) + out[0:per, 0:LANES]
        design[pl.ds(PITCH * k, per), :] = conv
        return 0

    lax.fori_loop(0, bases, convolve_cols, 0, unroll=bases)
    science = jnp.concatenate([arrived_ref[pl.ds(start + PARCEL * b, SUBS), :] for b in range(VISITS)], axis=0)
    design[PITCH * bases : PITCH * bases + per, :] = jnp.ones((per, LANES), F32)
    design[PITCH * columns : PITCH * columns + per, :] = science
    design[PITCH * (columns + 1) :, :] = jnp.zeros((design.shape[0] - PITCH * (columns + 1), LANES), F32)

    def gram_of(b, _):
        left, right = [], []
        for q in range(SUBS):
            high, low = split(design[pl.ds(SUBS * b + q, 32, stride=PITCH), :])
            hit = jnp.broadcast_to(weight[pl.ds(SUBS * b + q, 1), :], (2 * SUBS, LANES)).astype(BF16)
            both = jnp.concatenate([high, low], axis=0)
            left.append(jnp.concatenate([both[16 * i : 16 * (i + 1)] * hit for i in range(4)], axis=0))
            right.append(both)
            pairs[b, 32 * q : 32 * (q + 1), 0:LANES] = high
            pairs[b, 32 * q : 32 * (q + 1), LANES:] = low
        left = jnp.concatenate(left, axis=1)
        right = jnp.concatenate(right, axis=1)
        out = lax.dot_general(left, right, NT, preferred_element_type=F32)
        halves = out[32:64] + out[0:32]
        gram[pl.ds(b, 32, stride=VISITS), :] = jnp.concatenate([halves, jnp.zeros((32, LANES - 64), F32)], axis=1)
        return 0

    lax.fori_loop(0, VISITS, gram_of, 0, unroll=VISITS)

    groups = [gram[per * g : per * (g + 1), :].T for g in range(4)]
    groups = [group[0:32] + group[32:64] for group in groups]
    lane = iota((32, LANES), 1)
    sub = iota((32, LANES), 0)
    for g in range(4):
        diagonal = (sub == 8 * g + lane // VISITS) & (sub < columns)
        groups[g] = groups[g] + jnp.where(diagonal, RIDGE, 0.0)
    visit = lane % VISITS

    def spread(p):
        ends = min(SUBS * (p + 1), columns + 1)
        return {j: jnp.take_along_axis(groups[p], visit + VISITS * (j - SUBS * p), axis=1) for j in range(SUBS * p, ends)}

    scale = jnp.zeros((32, LANES), F32)
    panel = spread(0)
    for k in range(columns):
        p = k // SUBS
        if k % SUBS == SUBS - AHEAD and p < 3:
            panel.update(spread(p + 1))
        here = sub == k
        column = panel.pop(k)
        inverse = 1.0 / column[k : k + 1, :]
        scaled = jnp.where(here, 0.0, column * inverse)
        scale = jnp.where(here, inverse, scale)
        for j in panel:
            panel[j] = panel[j] - scaled * panel[j][k : k + 1, :]
        for g in range(p + 1, 4):
            if SUBS * g not in panel:
                groups[g] = groups[g] - scaled * groups[g][k : k + 1, :]
    answer = panel[columns] * scale
    tiled = jnp.concatenate([answer] * 4, axis=0).T

    row = iota((SUBS, LANES), 0)
    side = iota((SUBS, LANES), 1) // 32
    for b in range(VISITS):
        own_rows = jnp.broadcast_to(tiled[b : b + 1], (SUBS, LANES))
        spread = jnp.concatenate([jnp.where(side == row, own_rows, 0.0), jnp.where(side + 4 == row, own_rows, 0.0)], axis=1)
        high = spread.astype(BF16).astype(F32)
        terms = jnp.concatenate([high, spread - high], axis=0).astype(BF16)
        out = lax.dot_general(terms, pairs[b], (((1,), (0,)), ((), ())), preferred_element_type=F32)
        model = (out[0:SUBS, LANES:] + out[SUBS:, 0:LANES]) + out[0:SUBS, 0:LANES]
        out_ref[group * VISITS + b] = science[SUBS * b : SUBS * (b + 1)] - model


def unpack_kernel(slot_ref, back_ref, out_ref):
    strips = out_ref.shape[0]
    half = SUBS // CAP

    def pick(s, _):
        slot = slot_ref[s]
        both = back_ref[slot // CAP]
        out_ref[s] = jnp.where(slot % CAP == 0, both[0:half], both[half:SUBS])
        return 0

    lax.fori_loop(0, strips, pick, 0, unroll=min(strips, 16))


VMEM = pl.BlockSpec(memory_space=pltpu.VMEM)
SMEM = pl.BlockSpec(memory_space=pltpu.SMEM)
ANY = pl.BlockSpec(memory_space=pl.ANY)


def on_device(
    template, science, dest, row_offset, col_block, basis_rows, basis_cols, stamp_rows, stamp_cols
):
    peers = lax.axis_size("patch")
    rows, cols = template.shape
    strips, strip_rows, block_cols = science.shape
    bases = basis_rows.shape[0]
    blocks = cols // LANES
    height = rows + HEIGHT
    targets = dest.reshape(strips)

    kept = pltpu.VMEM if peers <= VISITS else jax.ShapeDtypeStruct
    payload, slots = pl.pallas_call(
        pack_kernel,
        out_shape=(kept((peers * PARCEL, LANES), F32), pltpu.SMEM((strips,), jnp.int32)),
        in_specs=[ANY, ANY, ANY, ANY, ANY],
        out_specs=(VMEM, SMEM),
        scratch_shapes=[
            pltpu.SMEM((strips,), jnp.int32),
            pltpu.SMEM((strips,), jnp.int32),
            pltpu.SMEM((strips,), jnp.int32),
            pltpu.VMEM((2 * rows, LANES), F32),
            pltpu.VMEM((strips, strip_rows, block_cols), F32),
            pltpu.SMEM((peers,), jnp.int32),
            pltpu.SMEM((CAP * peers,), jnp.int32),
            pltpu.SemaphoreType.DMA((6,)),
        ],
        name="pack",
    )(targets, row_offset, col_block, template, science)

    parcels = payload.reshape(peers, 1, PARCEL * LANES)
    arrived = lax.all_to_all(parcels, "patch", split_axis=0, concat_axis=0, tiled=True).reshape(payload.shape)

    frame, col_taps, beyond, row_taps, mask = pl.pallas_call(
        prep_kernel,
        out_shape=(
            pltpu.VMEM(((blocks + 1) * height, LANES), F32),
            pltpu.VMEM((bases, 2 * LANES, LANES), BF16),
            pltpu.VMEM((bases, 64, LANES), BF16),
            pltpu.VMEM((bases * SUBS, 2 * LANES), BF16),
            pltpu.VMEM((blocks * height, LANES), F32),
        ),
        in_specs=[VMEM, VMEM, VMEM, VMEM, VMEM],
        out_specs=(VMEM, VMEM, VMEM, VMEM, VMEM),
        scratch_shapes=[pltpu.VMEM((32, LANES), F32), pltpu.VMEM((LANES, LANES), F32)],
        name="prep",
    )(template, basis_rows.T, basis_cols.T, stamp_rows, stamp_cols)

    per = VISITS * SUBS
    residual, _ = pl.pallas_call(
        main_kernel,
        in_specs=[VMEM, VMEM, VMEM, VMEM, VMEM, VMEM],
        out_specs=(VMEM, VMEM),
        scratch_shapes=[
            pltpu.VMEM((per, LANES), F32),
            pltpu.VMEM((bases, per, 2 * LANES), F32),
            pltpu.VMEM((32 * PITCH, LANES), F32),
            pltpu.VMEM((VISITS, 2 * LANES, 2 * LANES), BF16),
            pltpu.VMEM((VISITS * 32, LANES), F32),
        ],
        out_shape=(jax.ShapeDtypeStruct((peers, SUBS, LANES), F32), pltpu.VMEM(((blocks + 1) * height, LANES), F32)),
        input_output_aliases={1: 1},
        compiler_params=pltpu.CompilerParams(vmem_limit_bytes=24 << 20),
        name="fit",
    )(arrived, frame, col_taps, beyond, row_taps, mask)

    returned = lax.all_to_all(residual, "patch", split_axis=0, concat_axis=0, tiled=True)

    return pl.pallas_call(
        unpack_kernel,
        out_shape=jax.ShapeDtypeStruct(science.shape, F32),
        in_specs=[SMEM, VMEM],
        out_specs=VMEM,
        compiler_params=pltpu.CompilerParams(vmem_limit_bytes=8 << 20),
        name="unpack",
    )(slots, returned)


def solution(mesh):
    placed = (
        P(None, ("groups", "patch")),
        P(("groups", "patch"), None, None),
        P(("groups", "patch"), None),
        P(("groups", "patch")),
        P(("groups", "patch")),
        P(),
        P(),
        P("groups", None),
        P("groups", None),
    )
    return jax.shard_map(
        on_device,
        mesh=mesh,
        in_specs=placed,
        out_specs=P(("groups", "patch"), None, None),
        check_vma=False,
    )
```

```python
import jax
import jax.numpy as jnp
from jax import lax
from jax.experimental import pallas as pl
from jax.experimental.pallas import tpu as pltpu
from jax.sharding import PartitionSpec as P

CAP = 2
STAMP_HALF = 10
RIDGE = 1.0
LANES = 128
SUBS = 8
VISITS = 16
PITCH = VISITS * SUBS + 1

F32 = jnp.float32
BF16 = jnp.bfloat16
NT = (((1,), (1,)), ((), ()))


def iota(shape, dim):
    return lax.broadcasted_iota(jnp.int32, shape, dim)


def split(x):
    high = x.astype(BF16)
    return high, (x - high.astype(F32)).astype(BF16)


PARCEL = 14
SHIFT = 10
TOP = 16
AHEAD = 4
HEIGHT = 40


def pack_kernel(
    dest_hbm, row_hbm, col_hbm, template_hbm, science_hbm, out_ref, slot_ref,
    dest_ref, row_ref, col_ref, edge, science_ref, count, source, sems,
):
    peers = out_ref.shape[0] // PARCEL
    strips = science_ref.shape[0]
    own = lax.axis_index("patch")
    rows = LANES // 2
    last = template_hbm.shape[1] - LANES
    copies = [
        pltpu.make_async_copy(source_ref, target_ref, sems.at[i])
        for i, (source_ref, target_ref) in enumerate(
            (
                (dest_hbm, dest_ref),
                (template_hbm.at[:, 0:LANES], edge.at[0:rows]),
                (template_hbm.at[:, last : last + LANES], edge.at[rows : 2 * rows]),
                (row_hbm, row_ref),
                (col_hbm, col_ref),
                (science_hbm, science_ref),
            )
        )
    ]
    for copy in copies:
        copy.start()

    def clear(d, _):
        count[d] = 0
        for r in range(CAP):
            source[CAP * d + r] = -1
        return 0

    lax.fori_loop(0, peers, clear, 0, unroll=min(peers, 16))

    def place(s, _):
        d = dest_ref[s]
        rank = count[d]
        source[CAP * d + rank] = s
        slot_ref[s] = CAP * d + rank
        count[d] = rank + 1
        return 0

    copies[0].wait()
    lax.fori_loop(0, strips, place, 0, unroll=min(strips, 16))
    for copy in copies[1:]:
        copy.wait()

    edges = edge[...].T
    lane = iota((SUBS, LANES), 1)
    sub = iota((SUBS, LANES), 0)
    low = lane < rows
    head = jnp.where(low, edges[0:8], pltpu.roll(edges[5:13], rows, 1))
    tail = jnp.where(low, pltpu.roll(edges[118:126], rows, 1), jnp.concatenate([edges[123:128], edges[0:3]], axis=0))
    info_here = sub == PARCEL - 1 - SUBS

    def fill(d, _):
        halo = jnp.where(d == own + 1, tail, head)
        info = jnp.zeros((SUBS, LANES), F32)
        parts = []
        for r in range(CAP):
            s = source[CAP * d + r]
            live = s >= 0
            at = jnp.maximum(s, 0)
            strip = science_ref[at]
            parts.append(jnp.where(live, strip, 0.0))
            values = (row_ref[at], col_ref[at], jnp.int32(1))
            for j, value in enumerate(values):
                value = jnp.where(live, value, 0).astype(F32)
                info = jnp.where(lane == 3 * r + j, value, info)
        out_ref[pl.ds(PARCEL * d, SUBS), :] = jnp.concatenate(parts, axis=0)
        out_ref[pl.ds(PARCEL * d + SUBS, PARCEL - SUBS), :] = jnp.where(info_here, info, halo)[0 : PARCEL - SUBS]
        return 0

    lax.fori_loop(0, peers, fill, 0, unroll=min(peers, 16))


def prep_kernel(
    template_ref, rows_ref, cols_ref, stamp_r_ref, stamp_c_ref, frame_ref, col_taps_ref, beyond_ref, row_taps_ref, mask_ref, pad_c, pad_t
):
    taps, bases = rows_ref.shape
    own = lax.axis_index("patch")
    rows = template_ref.shape[0]
    height = rows + HEIGHT
    blocks = frame_ref.shape[0] // height
    starts = iota((rows, LANES), 1) < SHIFT
    before = jnp.zeros((rows, LANES), F32)
    for c in range(blocks):
        here = jnp.zeros((rows, LANES), F32)
        if c < blocks - 1:
            here = pltpu.roll(template_ref[:, LANES * c : LANES * (c + 1)], SHIFT, 1)
        at = height * c
        frame_ref[at : at + TOP, :] = jnp.zeros((TOP, LANES), F32)
        frame_ref[at + TOP : at + TOP + rows, :] = jnp.where(starts, before, here)
        frame_ref[at + TOP + rows : at + height, :] = jnp.zeros((HEIGHT - TOP, LANES), F32)
        before = here
    sub_rows = rows
    blocks = blocks - 1
    sub_cols = blocks * LANES
    centre_r = stamp_r_ref[pl.ds(own, 1), :]
    centre_c = stamp_c_ref[pl.ds(own, 1), :]
    stamps = centre_r.shape[1]
    row_hit = (jnp.abs(iota((sub_rows, stamps), 0) - centre_r) <= STAMP_HALF).astype(F32).astype(BF16)
    col_hit = (jnp.abs(iota((sub_cols, stamps), 0) - centre_c) <= STAMP_HALF).astype(F32).astype(BF16)
    counts = lax.dot_general(row_hit, col_hit, NT, preferred_element_type=F32)
    for c in range(blocks):
        at = height * c
        mask_ref[at : at + height, :] = jnp.zeros((height, LANES), F32)
        mask_ref[at + TOP - SHIFT : at + TOP - SHIFT + rows, :] = jnp.minimum(counts[:, LANES * c : LANES * (c + 1)], 1.0)
    pad_t[...] = jnp.zeros_like(pad_t)
    for j in range(taps):
        at = -j % LANES
        pad_t[at : at + 1, 0:bases] = cols_ref[j : j + 1, :]
    pad_t[32 : 32 + taps, 0:bases] = rows_ref[...]
    filters = pad_t[...].T
    lane = iota((32, LANES), 1)
    pad_c[...] = jnp.where((lane == 0) | (lane > LANES - taps), filters[0:32], 0.0)
    full = jnp.where(iota((32, LANES), 1) < 32, pltpu.roll(filters[0:32], LANES - 32, 1), 0.0)
    high = full.astype(BF16).astype(F32)
    base = high + pltpu.roll(high, 32, 1) + pltpu.roll(full - high, 64, 1)
    wide = jnp.concatenate([base, jnp.zeros_like(base)], axis=1)
    lower = iota((SUBS, 2 * LANES), 0) < SUBS // CAP
    tiles = []
    for k in range(bases):
        row = jnp.broadcast_to(wide[k : k + 1, :], (SUBS, 2 * LANES))
        row = pltpu.roll(row, 0, 1, stride=1, stride_axis=0)
        row = jnp.where(lower, row, pltpu.roll(row, 96 - SUBS // CAP, 1))
        tiles.append(row)
    row_taps_ref[...] = jnp.concatenate(tiles, axis=0).astype(BF16)
    within = iota((LANES, LANES), 1) <= iota((LANES, LANES), 0)

    def column(k, _):
        ring = jnp.broadcast_to(pad_c[pl.ds(k, 1), :], (LANES, LANES))
        ring = pltpu.roll(ring, 0, 1, stride=1, stride_axis=0)
        high, low = split(jnp.where(within, ring, 0.0))
        col_taps_ref[k, :, 0:LANES] = high
        col_taps_ref[k, :, LANES:] = low
        high, low = split(jnp.where(within, 0.0, ring)[0:32])
        beyond_ref[k, :, 0:LANES] = high
        beyond_ref[k, :, LANES:] = low
        return 0

    lax.fori_loop(0, bases, column, 0, unroll=9)


def main_kernel(
    arrived_ref, frame_ref, col_taps_ref, beyond_ref, row_taps_ref, mask_ref, out_ref, frame,
    weight, field, design, pairs, gram,
):
    own = lax.axis_index("patch")
    peers = out_ref.shape[0]
    bases = col_taps_ref.shape[0]
    rows = LANES // 2
    last = frame.shape[0] - rows - HEIGHT
    per = VISITS * SUBS

    skip = PARCEL - SUBS
    left = arrived_ref[pl.ds(PARCEL * jnp.maximum(own - 1, 0) + skip, SUBS), :]
    right = arrived_ref[pl.ds(PARCEL * jnp.minimum(own + 1, peers - 1) + skip, SUBS), :]
    left = jnp.where(own > 0, left, 0.0)
    right = jnp.where(own < peers - 1, right, 0.0)
    pick = slice(SUBS - skip, SUBS - 1)
    ends = [tile[pick] for tile in (pltpu.roll(right, rows, 1), right, left, pltpu.roll(left, rows, 1))]
    gap = jnp.zeros((LANES - 2 * SHIFT, LANES), F32)
    halo = jnp.concatenate([ends[0], ends[1], gap, ends[2], ends[3]], axis=0).T
    halo = pltpu.roll(halo, SHIFT, 1)
    starts = iota((rows, LANES), 1) < SHIFT
    first_rows = slice(TOP, TOP + rows)
    last_rows = slice(last + TOP, last + TOP + rows)
    frame[first_rows, :] = jnp.where(starts, halo[0:rows], frame_ref[first_rows, :])
    frame[last_rows, :] = jnp.where(starts, frame_ref[last_rows, :], halo[rows : 2 * rows])

    def fit_group(group, _):
        fit_visits(
            group, arrived_ref, col_taps_ref, beyond_ref, row_taps_ref, mask_ref, out_ref,
            frame, weight, field, design, pairs, gram,
        )
        return 0

    if peers == VISITS:
        fit_group(0, 0)
    else:
        lax.fori_loop(0, peers // VISITS, fit_group, 0)


def fit_visits(
    group, arrived_ref, col_taps_ref, beyond_ref, row_taps_ref, mask_ref, out_ref,
    frame, weight, field, design, pairs, gram,
):
    bases = col_taps_ref.shape[0]
    columns = bases + 1
    per = VISITS * SUBS
    row_taps = row_taps_ref[:, 0:192]

    height = LANES // 2 + HEIGHT
    start = group * (VISITS * PARCEL)
    info = arrived_ref[pl.ds(start + PARCEL - 1, VISITS, stride=PARCEL), :]
    block = pltpu.roll(info, LANES - 1, 1)
    live = pltpu.roll(info, LANES - 2, 1)
    places = jnp.where(live > 0.0, block * height + info + (TOP - SHIFT), height - 32.0).astype(jnp.int32)

    first = [[places[b, 3 * r] for r in range(CAP)] for b in range(VISITS)]

    def tall(windows):
        terms = []
        for window in windows:
            high, low = split(window)
            terms += [high, low, high]
        return jnp.concatenate(terms, axis=0)

    for b in range(0, VISITS, 2):
        pair = []
        for v in (b, b + 1):
            masks = [mask_ref[pl.ds(at, SUBS), :][0 : SUBS // CAP] for at in first[v]]
            weight[SUBS * v : SUBS * (v + 1), :] = jnp.concatenate(masks, axis=0)
            pair.append(tall([frame[pl.ds(at, 32), :] for at in first[v]]))
        across = jnp.dot(row_taps, jnp.concatenate(pair, axis=1), preferred_element_type=F32)
        for k in range(bases):
            rows = across[SUBS * k : SUBS * (k + 1)]
            field[k, SUBS * b : SUBS * (b + 1), 0:LANES] = rows[:, 0:LANES]
            field[k, SUBS * (b + 1) : SUBS * (b + 2), 0:LANES] = rows[:, LANES:]

    place_of = iota((32, LANES), 1) // 32
    for b in range(0, VISITS, 8):
        sides = []
        for h in range(b, b + 8, 4):
            windows = []
            for r in range(CAP):
                window = frame[pl.ds(first[h][r] + height, 32), :]
                for v in range(1, 4):
                    moved = pltpu.roll(frame[pl.ds(first[h + v][r] + height, 32), :], 32 * v, 1)
                    window = jnp.where(place_of == v, moved, window)
                windows.append(window)
            sides.append(tall(windows))
        across = jnp.dot(row_taps, jnp.concatenate(sides, axis=1), preferred_element_type=F32)
        for k in range(bases):
            for v in range(8):
                rows = across[SUBS * k : SUBS * (k + 1), LANES * (v // 4) : LANES * (v // 4 + 1)]
                rows = jnp.where(place_of[0:SUBS] == v % 4, rows, 0.0)
                field[k, SUBS * (b + v) : SUBS * (b + v + 1), LANES:] = rows

    none = jnp.zeros((LANES, LANES), BF16)

    def convolve_cols(k):
        high, low = split(field[k, :, 0:LANES])
        tail = field[k, :, LANES:]
        tail_high = tail.astype(BF16).astype(F32)
        rest = pltpu.roll(tail - tail_high, 32, 1)
        terms = jnp.concatenate([high, (tail_high + rest).astype(BF16)], axis=1)
        taps = jnp.concatenate([col_taps_ref[k]] + [beyond_ref[k]] * 4, axis=0)
        out = jnp.dot(terms, taps, preferred_element_type=F32)
        return low, out[:, 0:LANES] + out[:, LANES:]

    for k in range(0, bases, 2):
        low, conv = convolve_cols(k)
        taps = col_taps_ref[k, :, 0:LANES]
        if k + 1 == bases:
            rest = jnp.dot(low, taps, preferred_element_type=F32)
        else:
            next_low, next_conv = convolve_cols(k + 1)
            next_taps = col_taps_ref[k + 1, :, 0:LANES]
            lows = jnp.concatenate([low, next_low], axis=1)
            block = jnp.concatenate(
                [jnp.concatenate([taps, none], axis=1), jnp.concatenate([none, next_taps], axis=1)], axis=0
            )
            rest = jnp.dot(lows, block, preferred_element_type=F32)
            design[PITCH * (k + 1) : PITCH * (k + 1) + per, :] = next_conv + rest[:, LANES:]
        design[PITCH * k : PITCH * k + per, :] = conv + rest[:, 0:LANES]
    science = jnp.concatenate([arrived_ref[pl.ds(start + PARCEL * b, SUBS), :] for b in range(VISITS)], axis=0)
    design[PITCH * bases : PITCH * bases + per, :] = jnp.ones((per, LANES), F32)
    design[PITCH * columns : PITCH * columns + per, :] = science
    design[PITCH * (columns + 1) :, :] = jnp.zeros((design.shape[0] - PITCH * (columns + 1), LANES), F32)

    def gram_of(b, _):
        left, right = [], []
        for q in range(SUBS):
            high, low = split(design[pl.ds(SUBS * b + q, 32, stride=PITCH), :])
            hit = jnp.broadcast_to(weight[pl.ds(SUBS * b + q, 1), :], (2 * SUBS, LANES)).astype(BF16)
            both = jnp.concatenate([high, low], axis=0)
            left.append(jnp.concatenate([both[16 * i : 16 * (i + 1)] * hit for i in range(4)], axis=0))
            right.append(both)
            pairs[b, 32 * q : 32 * (q + 1), 0:LANES] = high
            pairs[b, 32 * q : 32 * (q + 1), LANES:] = low
        left = jnp.concatenate(left, axis=1)
        right = jnp.concatenate(right, axis=1)
        out = lax.dot_general(left, right, NT, preferred_element_type=F32)
        halves = out[32:64] + out[0:32]
        gram[pl.ds(b, 32, stride=VISITS), :] = jnp.concatenate([halves, jnp.zeros((32, LANES - 64), F32)], axis=1)
        return 0

    lax.fori_loop(0, VISITS, gram_of, 0, unroll=VISITS)

    groups = [gram[per * g : per * (g + 1), :].T for g in range(4)]
    groups = [group[0:32] + group[32:64] for group in groups]
    lane = iota((32, LANES), 1)
    sub = iota((32, LANES), 0)
    for g in range(4):
        diagonal = (sub == 8 * g + lane // VISITS) & (sub < columns)
        groups[g] = groups[g] + jnp.where(diagonal, RIDGE, 0.0)
    visit = lane % VISITS

    def spread(p):
        ends = min(SUBS * (p + 1), columns + 1)
        return {j: jnp.take_along_axis(groups[p], visit + VISITS * (j - SUBS * p), axis=1) for j in range(SUBS * p, ends)}

    scale = jnp.zeros((32, LANES), F32)
    panel = spread(0)
    for k in range(columns):
        p = k // SUBS
        if k % SUBS == SUBS - AHEAD and p < 3:
            panel.update(spread(p + 1))
        here = sub == k
        column = panel.pop(k)
        inverse = 1.0 / column[k : k + 1, :]
        scaled = jnp.where(here, 0.0, column * inverse)
        scale = jnp.where(here, inverse, scale)
        for j in panel:
            panel[j] = panel[j] - scaled * panel[j][k : k + 1, :]
        for g in range(p + 1, 4):
            if SUBS * g not in panel:
                groups[g] = groups[g] - scaled * groups[g][k : k + 1, :]
    answer = panel[columns] * scale
    tiled = jnp.concatenate([answer] * 4, axis=0).T

    row = iota((SUBS, LANES), 0)
    side = iota((SUBS, LANES), 1) // 32
    for b in range(VISITS):
        own_rows = jnp.broadcast_to(tiled[b : b + 1], (SUBS, LANES))
        spread = jnp.concatenate([jnp.where(side == row, own_rows, 0.0), jnp.where(side + 4 == row, own_rows, 0.0)], axis=1)
        high = spread.astype(BF16).astype(F32)
        terms = jnp.concatenate([high, spread - high], axis=0).astype(BF16)
        out = lax.dot_general(terms, pairs[b], (((1,), (0,)), ((), ())), preferred_element_type=F32)
        model = (out[0:SUBS, LANES:] + out[SUBS:, 0:LANES]) + out[0:SUBS, 0:LANES]
        out_ref[group * VISITS + b] = science[SUBS * b : SUBS * (b + 1)] - model


def unpack_kernel(slot_ref, back_ref, out_ref):
    strips = out_ref.shape[0]
    half = SUBS // CAP

    def pick(s, _):
        slot = slot_ref[s]
        both = back_ref[slot // CAP]
        out_ref[s] = jnp.where(slot % CAP == 0, both[0:half], both[half:SUBS])
        return 0

    lax.fori_loop(0, strips, pick, 0, unroll=min(strips, 16))


VMEM = pl.BlockSpec(memory_space=pltpu.VMEM)
SMEM = pl.BlockSpec(memory_space=pltpu.SMEM)
ANY = pl.BlockSpec(memory_space=pl.ANY)


def on_device(
    template, science, dest, row_offset, col_block, basis_rows, basis_cols, stamp_rows, stamp_cols
):
    peers = lax.axis_size("patch")
    rows, cols = template.shape
    strips, strip_rows, block_cols = science.shape
    bases = basis_rows.shape[0]
    blocks = cols // LANES
    height = rows + HEIGHT
    targets = dest.reshape(strips)

    kept = pltpu.VMEM if peers <= VISITS else jax.ShapeDtypeStruct
    payload, slots = pl.pallas_call(
        pack_kernel,
        out_shape=(kept((peers * PARCEL, LANES), F32), pltpu.SMEM((strips,), jnp.int32)),
        in_specs=[ANY, ANY, ANY, ANY, ANY],
        out_specs=(VMEM, SMEM),
        scratch_shapes=[
            pltpu.SMEM((strips,), jnp.int32),
            pltpu.SMEM((strips,), jnp.int32),
            pltpu.SMEM((strips,), jnp.int32),
            pltpu.VMEM((2 * rows, LANES), F32),
            pltpu.VMEM((strips, strip_rows, block_cols), F32),
            pltpu.SMEM((peers,), jnp.int32),
            pltpu.SMEM((CAP * peers,), jnp.int32),
            pltpu.SemaphoreType.DMA((6,)),
        ],
        name="pack",
    )(targets, row_offset, col_block, template, science)

    parcels = payload.reshape(peers, 1, PARCEL * LANES)
    arrived = lax.all_to_all(parcels, "patch", split_axis=0, concat_axis=0, tiled=True).reshape(payload.shape)

    frame, col_taps, beyond, row_taps, mask = pl.pallas_call(
        prep_kernel,
        out_shape=(
            pltpu.VMEM(((blocks + 1) * height, LANES), F32),
            pltpu.VMEM((bases, LANES, 2 * LANES), BF16),
            pltpu.VMEM((bases, 32, 2 * LANES), BF16),
            pltpu.VMEM((bases * SUBS, 2 * LANES), BF16),
            pltpu.VMEM((blocks * height, LANES), F32),
        ),
        in_specs=[VMEM, VMEM, VMEM, VMEM, VMEM],
        out_specs=(VMEM, VMEM, VMEM, VMEM, VMEM),
        scratch_shapes=[pltpu.VMEM((32, LANES), F32), pltpu.VMEM((LANES, LANES), F32)],
        name="prep",
    )(template, basis_rows.T, basis_cols.T, stamp_rows, stamp_cols)

    per = VISITS * SUBS
    residual, _ = pl.pallas_call(
        main_kernel,
        in_specs=[VMEM, VMEM, VMEM, VMEM, VMEM, VMEM],
        out_specs=(VMEM, VMEM),
        scratch_shapes=[
            pltpu.VMEM((per, LANES), F32),
            pltpu.VMEM((bases, per, 2 * LANES), F32),
            pltpu.VMEM((32 * PITCH, LANES), F32),
            pltpu.VMEM((VISITS, 2 * LANES, 2 * LANES), BF16),
            pltpu.VMEM((VISITS * 32, LANES), F32),
        ],
        out_shape=(jax.ShapeDtypeStruct((peers, SUBS, LANES), F32), pltpu.VMEM(((blocks + 1) * height, LANES), F32)),
        input_output_aliases={1: 1},
        compiler_params=pltpu.CompilerParams(vmem_limit_bytes=24 << 20),
        name="fit",
    )(arrived, frame, col_taps, beyond, row_taps, mask)

    returned = lax.all_to_all(residual, "patch", split_axis=0, concat_axis=0, tiled=True)

    return pl.pallas_call(
        unpack_kernel,
        out_shape=jax.ShapeDtypeStruct(science.shape, F32),
        in_specs=[SMEM, VMEM],
        out_specs=VMEM,
        compiler_params=pltpu.CompilerParams(vmem_limit_bytes=8 << 20),
        name="unpack",
    )(slots, returned)


def solution(mesh):
    placed = (
        P(None, ("groups", "patch")),
        P(("groups", "patch"), None, None),
        P(("groups", "patch"), None),
        P(("groups", "patch")),
        P(("groups", "patch")),
        P(),
        P(),
        P("groups", None),
        P("groups", None),
    )
    return jax.shard_map(
        on_device,
        mesh=mesh,
        in_specs=placed,
        out_specs=P(("groups", "patch"), None, None),
        check_vma=False,
    )
```
